512 devices in a mesh: dom: 512 (over z, y, x, core).
Axes of the slice: x: 4, y: 4, z: 16, core: 2. Of those that a mesh axis runs over, the one named last changes fastest.
Arguments:
- features: bfloat16 [131072, 256], P('dom'), may hold values from -48 to 48
- w_query: bfloat16 [256, 256], replicated, may hold values from -0.375 to 0.375
- w_key: bfloat16 [256, 256], replicated, may hold values from -0.375 to 0.375
- w_value: bfloat16 [256, 256], replicated, may hold values from -0.375 to 0.375
- w_out: bfloat16 [256, 256], replicated, may hold values from -0.375 to 0.375
- local_blocks: int32 [1024, 4], P('dom'), may hold values from 0 to 3, as said below
- local_count: int32 [1024], P('dom'), may hold values from 1 to 4, as said below
- expander_blocks: int32 [4, 1024, 2], P(None, 'dom'), may hold values from 0 to 1, as said below
- expander_count: int32 [4, 1024], P(None, 'dom'), may hold values from 1 to 2, as said below
Outputs:
- updated: bfloat16 [131072, 256], P('dom')
The draws below stay inside these ranges and needn't reach their ends.
Inputs may be any that keep to these rules, and one draw needn't show every extreme that they name: `local_blocks`: each row names 4 different positions of the extended range; the row of each partition's first block begins with position 0 and that of its last block with position 3. `local_count`: loads differ from partition to partition; block 0 of every partition uses its partition's largest count. `expander_blocks`: each row names 2 different blocks. `expander_count`: loads differ from partition to partition; block 0 of every partition uses its partition's largest count.
All inputs are finite; a program needn't handle non-finite values.
Results may differ from the reference program's by a relative error of at most 0.0065.
Values may be sent and summed in bfloat16 or wider, within the bound.
A program may use at most 64 MiB of HBM per device.

```python
import jax
import jax.numpy as jnp
from jax import lax

D = 256
HEADS = 8
BLK = 128
NB = 2
MAXL = 4
MAXE = 2
MATCH = 4
BLOCKS = 1024
NODES = 131072
N_DOM = 512


def ragged_counts(key, most):
    key_dev, key_blk = jax.random.split(key)
    device_total = BLOCKS // NB
    ceiling = jax.random.randint(key_dev, (device_total,), 1, most + 1).at[0].set(most)
    spread = jax.random.randint(key_blk, (device_total, NB), 0, 1 << 20)
    counts = 1 + spread * ceiling[:, None] // (1 << 20)
    counts = counts.at[:, 0].set(ceiling)
    return counts.reshape(BLOCKS).astype(jnp.int32)


def distinct_rows(key, row_total, choose_from, keep):
    row_keys = jax.random.split(key, row_total)
    picked = jax.vmap(lambda single: jax.random.permutation(single, choose_from)[:keep])(row_keys)
    return picked.astype(jnp.int32)


def draw_local_blocks(key, part):
    row_keys = jax.random.split(jax.random.fold_in(key, 17), BLOCKS)
    ranks = jax.vmap(lambda single: jax.random.permutation(single, NB + 2))(row_keys).astype(jnp.int32)
    within = jnp.arange(BLOCKS, dtype=jnp.int32) % NB
    position = jnp.arange(NB + 2, dtype=jnp.int32)
    first_row = (within == 0)[:, None] & (position == 0)[None, :]
    last_row = (within == NB - 1)[:, None] & (position == NB + 1)[None, :]
    ranks = jnp.where(first_row | last_row, jnp.int32(-1), ranks)
    order = jnp.argsort(ranks, axis=1, stable=True)
    return order[:, :MAXL].astype(jnp.int32)


def draw_local_count(key, part):
    return ragged_counts(jax.random.fold_in(key, 11), MAXL)


def draw_expander_blocks(key, part):
    picked = distinct_rows(jax.random.fold_in(key, 19), MATCH * BLOCKS, NB, MAXE)
    return picked.reshape(MATCH, BLOCKS, MAXE)


def draw_expander_count(key, part):
    match_keys = jax.random.split(jax.random.fold_in(key, 13), MATCH)
    return jnp.stack([ragged_counts(match_keys[m], MAXE) for m in range(MATCH)])


def draw_features(key, part):
    key_base = jax.random.fold_in(jax.random.fold_in(key, 23), 0)
    values = jnp.clip(jax.random.normal(key_base, (NODES, D), jnp.float32), -6.0, 6.0)
    return values.astype(jnp.bfloat16)


def centred(rng, shape, deviation, reach, kind=jnp.bfloat16):
    return jnp.clip(deviation * jax.random.normal(rng, shape, jnp.float32), -reach, reach).astype(kind)


def setup_inputs(seed: int = 0) -> dict:
    streams_of = jax.random.split(jax.random.key(seed), 10)
    return {
        "features": draw_features(jax.random.fold_in(streams_of[9], 71), 0),
        "w_query": centred(streams_of[1], (D, D), D ** -0.5, 0.375),
        "w_key": centred(streams_of[2], (D, D), D ** -0.5, 0.375),
        "w_value": centred(streams_of[3], (D, D), D ** -0.5, 0.375),
        "w_out": centred(streams_of[4], (D, D), D ** -0.5, 0.375),
        "local_blocks": draw_local_blocks(jax.random.fold_in(streams_of[9], 71), 0),
        "local_count": draw_local_count(jax.random.fold_in(streams_of[9], 71), 0),
        "expander_blocks": draw_expander_blocks(jax.random.fold_in(streams_of[9], 71), 0),
        "expander_count": draw_expander_count(jax.random.fold_in(streams_of[9], 71), 0),
    }


epsilon = 1e-06

def part_state(queries, kv_blocks, chosen, live_count):
    picked = kv_blocks[chosen].astype(jnp.float32)
    slot_count = chosen.shape[0]
    block_rows = kv_blocks.shape[1]
    picked = picked.reshape(slot_count * block_rows, 2, HEADS, D // HEADS)
    key_rows = picked[:, 0]
    values = picked[:, 1]
    scores = jnp.einsum('qhd,khd->hqk', queries.astype(jnp.float32), key_rows)
    usable = jnp.arange(slot_count * block_rows, dtype=jnp.int32) // block_rows < live_count
    scores = jnp.where(usable[None, None, :], scores, jnp.float32(-1e+30))
    row_max = lax.optimization_barrier(jnp.max(scores, axis=-1))
    weights = jnp.where(usable[None, None, :], jnp.exp(scores - row_max[..., None]), jnp.float32(0.0))
    weights = weights.astype(jnp.bfloat16).astype(jnp.float32)
    weight_sum = lax.optimization_barrier(jnp.sum(weights, axis=-1))
    context = jnp.einsum('hqk,khd->hqd', weights, values)
    return (row_max, weight_sum, context)

def combine(states):
    tops = jnp.stack([s[0] for s in states])
    sums = jnp.stack([s[1] for s in states])
    outs = jnp.stack([s[2] for s in states])
    highest = lax.optimization_barrier(jnp.max(tops, axis=0))
    factor = jnp.exp(tops - highest[None])
    total = lax.optimization_barrier(jnp.sum(factor * sums, axis=0))
    merged = lax.optimization_barrier(jnp.sum(factor[..., None] * outs, axis=0))
    return merged / total[..., None]

def reference(features, w_query, w_key, w_value, w_out, local_blocks, local_count, expander_blocks, expander_count):
    scaling = float(D // HEADS) ** (-0.5)
    queries = (jnp.dot(features, w_query, preferred_element_type=jnp.float32) * scaling).astype(jnp.bfloat16)
    queries = queries.reshape(N_DOM, NB, BLK, HEADS, D // HEADS)
    w_pair = jnp.concatenate([w_key, w_value], axis=1)
    pairs = jnp.dot(features, w_pair, preferred_element_type=jnp.float32).astype(jnp.bfloat16)
    pair_blocks = pairs.reshape(BLOCKS, BLK, 2 * D)
    pair_parts = pairs.reshape(N_DOM, NB, BLK, 2 * D)
    levels = N_DOM.bit_length() - 1
    node_index = jnp.arange(N_DOM, dtype=jnp.int32)
    partners = [jnp.bitwise_xor(node_index, jnp.int32(1 << m * levels // MATCH)) for m in range(MATCH)]

    def one_partition(part):
        ranged = (part * NB - 1 + jnp.arange(NB + 2, dtype=jnp.int32)) % BLOCKS
        extended = pair_blocks[ranged]
        remotes = [pair_parts[partners[m][part]] for m in range(MATCH)]

        def one_block(block):
            global_block = part * NB + block
            own_queries = queries[part, block]
            states = [part_state(own_queries, extended, local_blocks[global_block], local_count[global_block])]
            for m in range(MATCH):
                states.append(part_state(own_queries, remotes[m], expander_blocks[m, global_block], expander_count[m, global_block]))
            merged = combine(states)
            return jnp.transpose(merged, (1, 0, 2)).reshape(BLK, D).astype(jnp.bfloat16)
        return lax.map(one_block, jnp.arange(NB, dtype=jnp.int32))
    context = lax.map(one_partition, jnp.arange(N_DOM, dtype=jnp.int32)).reshape(NODES, D)
    mixed = jnp.dot(context, w_out, preferred_element_type=jnp.float32)
    normed = mixed / jnp.sqrt(lax.optimization_barrier(jnp.mean(mixed * mixed, axis=-1, keepdims=True)) + epsilon)
    return (features.astype(jnp.float32) + normed).astype(jnp.bfloat16)
```

```python
import functools

import jax
import jax.numpy as jnp
from jax import lax
from jax.experimental import pallas as pl
from jax.experimental.pallas import tpu as pltpu
from jax.sharding import PartitionSpec as P

HEADS = 8
BLK = 128
EPS = 1e-06
LOG2E = 1.4426950408889634
OFF = -1e30
FLOOR = -1e20
MESH = pl.DeviceIdType.MESH
F32 = jnp.float32
BF16 = jnp.bfloat16
CORE, XX, YY, HALO, ZZ = range(5)


def flip(me, apart):
    wide = 1 << apart
    return me + wide - 2 * wide * ((me // wide) % 2)


def dot(a, b, over):
    return lax.dot_general(a, b, ((over[0], over[1]), ((), ())), preferred_element_type=F32)


def attend_kernel(
    peers, swaps,
    f_hbm, wq_hbm, wk_hbm, wv_hbm, lb_hbm, lc_hbm, eb_hbm, ec_hbm,
    ctx_ref,
    own, wq, wk, wv, lb, lc, eb, ec,
    kv, g, wvt, vt, bias, top, acc,
    local_sem, send_sem, recv_sem, ready_sem,
):
    me = lax.axis_index("dom")
    odd = me % 2
    rows = own.shape[0]
    width = own.shape[1]
    head = width // HEADS
    beside = lax.rem(me + 2 * odd - 1 + peers, peers)
    partner = [flip(me, swaps[0]), flip(me, swaps[1]), flip(me, swaps[2]), beside, flip(me, swaps[3])]

    def waits(apart):
        low = 1 << apart
        usual = (me // low) % 2
        return jnp.where(me == 0, 1, jnp.where(me == low, 0, usual))

    even_end = me + odd
    late = [
        1 - odd,
        waits(swaps[1]),
        waits(swaps[2]),
        jnp.where(even_end % 8 == 0, odd, 1 - odd),
        waits(swaps[3]),
    ]

    barrier = pltpu.get_barrier_semaphore()
    for k in (ZZ, YY, XX, CORE, HALO):
        @pl.when(late[k] == 0)
        def _(k=k):
            pl.semaphore_signal(barrier, inc=1, device_id=(partner[k],), device_id_type=MESH)

    pulls = [
        pltpu.make_async_copy(src, dst, local_sem.at[i])
        for i, (src, dst) in enumerate(
            ((f_hbm, own), (wq_hbm, wq), (wk_hbm, wk), (wv_hbm, wv),
             (lb_hbm, lb), (lc_hbm, lc), (eb_hbm, eb), (ec_hbm, ec))
        )
    ]
    for pull in pulls:
        pull.start()

    def copies(k):
        if k == HALO:
            src = f_hbm.at[pl.ds(pl.multiple_of(odd * BLK, BLK), BLK)]
            dst = kv.at[k, pl.ds(0, BLK)]
        else:
            src, dst = f_hbm, kv.at[k]
        return pltpu.make_async_remote_copy(
            src_ref=src, dst_ref=dst, send_sem=send_sem.at[k], recv_sem=recv_sem.at[k],
            device_id=(partner[k],), device_id_type=MESH,
        )

    moves = [copies(k) for k in range(5)]
    greeted = late[0] + late[1] + late[2] + late[3] + late[4]

    @pl.when(greeted > 0)
    def _():
        pl.semaphore_wait(barrier, greeted)

    for k in (ZZ, YY, XX, CORE, HALO):
        @pl.when(late[k] == 1)
        def _(k=k):
            pl.semaphore_signal(ready_sem.at[k], inc=1, device_id=(partner[k],), device_id_type=MESH)
            moves[k].start()

    for i in range(4):
        pulls[i].wait()
    own_rows = own[...]
    scale = LOG2E * float(head) ** (-0.5)
    qt = (dot(wq[...], own_rows, ((0,), (1,))) * scale).astype(BF16)
    wvt[...] = wv[...].T
    for h in range(HEADS):
        parts = [qt[h * head:(h + 1) * head]]
        if h:
            parts.insert(0, jnp.zeros((h * head, rows), BF16))
        if h < HEADS - 1:
            parts.append(jnp.zeros((width - (h + 1) * head, rows), BF16))
        g[h] = dot(wk[...], jnp.concatenate(parts, axis=0), ((1,), (0,))).astype(BF16)

    for k in (CORE, HALO, XX, YY, ZZ):
        @pl.when(late[k] == 0)
        def _(k=k):
            pl.semaphore_wait(ready_sem.at[k], 1)
            moves[k].start()

    for i in range(4, 8):
        pulls[i].wait()

    def put(slot, block, counts):
        row = [
            jnp.full((1, BLK), jnp.where(c == 0, OFF, jnp.where(c == 1, 0.0, 1.0)).astype(F32))
            for c in counts
        ]
        bias[slot, pl.ds(block, 1), :] = jnp.concatenate(row, axis=1)

    def in_local(q, position):
        used = jnp.int32(0)
        for j in range(4):
            used += jnp.where((lb[q, j] == position) & (j < lc[q]), 1, 0)
        return used

    def in_match(m, q, block):
        used = jnp.int32(0)
        for j in range(2):
            used += jnp.where((eb[q, j, m] == block) & (j < ec[q, m]), 1, 0)
        return used

    near = [[in_local(q, j) for j in range(4)] for q in range(2)]
    for b in range(2):
        put(0, b, [near[q][1 + b] for q in range(2)])
        extra = [jnp.where(odd == b, near[q][0] if b else near[q][3], 0) for q in range(2)]
        put(1 + CORE, b, [in_match(0, q, b) + extra[q] for q in range(2)])
        for m, k in ((1, XX), (2, YY), (3, ZZ)):
            put(1 + k, b, [in_match(m, q, b) for q in range(2)])
    put(1 + HALO, 0, [jnp.where(odd == 1, near[q][3], near[q][0]) for q in range(2)])
    put(1 + HALO, 1, [jnp.int32(0)] * 2)

    kv[HALO, pl.ds(BLK, BLK), :] = jnp.zeros((BLK, width), BF16)
    for h in range(HEADS):
        vt[h, pl.ds(head, 16), :] = jnp.ones((16, rows), BF16)
    top[...] = jnp.full(top.shape, FLOOR, F32)
    acc[...] = jnp.zeros(acc.shape, F32)

    def part(keys, slot):
        values = dot(wvt[...], keys, ((1,), (1,))).astype(BF16)
        for h in range(HEADS):
            vt[h, pl.ds(0, head), :] = values[h * head:(h + 1) * head]
        for h in range(HEADS):
            scores = dot(keys, g[h], ((1,), (0,)))
            first = bias[slot, pl.ds(0, 1), :]
            second = bias[slot, pl.ds(1, 1), :]
            old = top[h]
            new = jnp.maximum(
                old,
                jnp.maximum(
                    jnp.max(scores[:BLK], axis=0, keepdims=True) + first,
                    jnp.max(scores[BLK:], axis=0, keepdims=True) + second,
                ),
            )
            top[h] = new
            weights = jnp.concatenate(
                [
                    jnp.exp2(scores[:BLK] - (new - first)).astype(BF16),
                    jnp.exp2(scores[BLK:] - (new - second)).astype(BF16),
                ],
                axis=0,
            )
            out = dot(vt[h], weights, ((1,), (0,)))
            acc[h] = acc[h] * jnp.exp2(old - new) + out[: head + 8]

    part(own_rows, 0)

    for k in range(5):
        moves[k].wait_recv()
        part(kv[k], k + 1)

    for h in range(HEADS):
        ctx_ref[pl.ds(h * head, head), :] = (
            acc[h, pl.ds(0, head), :] / acc[h, pl.ds(head, 1), :]
        ).astype(BF16)
    for k in range(5):
        moves[k].wait_send()


def finish_kernel(ctx_ref, f_ref, w_ref, o_ref):
    mixed = dot(ctx_ref[...], w_ref[...], ((0,), (0,)))
    mean = jnp.mean(mixed * mixed, axis=-1, keepdims=True)
    o_ref[...] = (f_ref[...].astype(F32) + mixed * lax.rsqrt(mean + EPS)).astype(BF16)


def shards(features, w_query, w_key, w_value, w_out, local_blocks, local_count, expander_blocks, expander_count):
    rows, width = features.shape
    head = width // HEADS
    peers = lax.axis_size("dom")
    levels = peers.bit_length() - 1
    matches = expander_blocks.shape[0]
    swaps = [m * levels // matches for m in range(matches)]
    whole = pl.BlockSpec(memory_space=pltpu.HBM)
    inside = pl.BlockSpec(memory_space=pltpu.VMEM)
    expander_blocks = jnp.transpose(expander_blocks, (1, 2, 0))
    expander_count = expander_count.T
    ctx = pl.pallas_call(
        functools.partial(attend_kernel, peers, swaps),
        out_shape=jax.ShapeDtypeStruct((width, rows), BF16),
        in_specs=[whole] * 8,
        out_specs=inside,
        scratch_shapes=[
            pltpu.VMEM((rows, width), BF16),
            pltpu.VMEM((width, width), BF16),
            pltpu.VMEM((width, width), BF16),
            pltpu.VMEM((width, width), BF16),
            pltpu.SMEM(local_blocks.shape, jnp.int32),
            pltpu.SMEM(local_count.shape, jnp.int32),
            pltpu.SMEM(expander_blocks.shape, jnp.int32),
            pltpu.SMEM(expander_count.shape, jnp.int32),
            pltpu.VMEM((5, rows, width), BF16),
            pltpu.VMEM((HEADS, width, rows), BF16),
            pltpu.VMEM((width, width), BF16),
            pltpu.VMEM((HEADS, head + 16, rows), BF16),
            pltpu.VMEM((6, 8, rows), F32),
            pltpu.VMEM((HEADS, 1, rows), F32),
            pltpu.VMEM((HEADS, head + 8, rows), F32),
            pltpu.SemaphoreType.DMA((8,)),
            pltpu.SemaphoreType.DMA((5,)),
            pltpu.SemaphoreType.DMA((5,)),
            pltpu.SemaphoreType.REGULAR((5,)),
        ],
        compiler_params=pltpu.CompilerParams(
            collective_id=0, has_side_effects=True
        ),
        name="attend",
    )(features, w_query, w_key, w_value, local_blocks, local_count, expander_blocks, expander_count)
    return pl.pallas_call(
        finish_kernel,
        out_shape=jax.ShapeDtypeStruct((rows, width), BF16),
        in_specs=[inside] * 3,
        out_specs=inside,
        compiler_params=pltpu.CompilerParams(vmem_limit_bytes=8 << 20),
        name="finish",
    )(ctx, features, w_out)


def solution(mesh):
    in_specs = (
        P("dom", None), P(), P(), P(), P(),
        P("dom", None), P("dom"), P(None, "dom", None), P(None, "dom"),
    )
    return jax.shard_map(
        shards, mesh=mesh, in_specs=in_specs, out_specs=P("dom", None), check_vma=False
    )
```

```python
import functools

import jax
import jax.numpy as jnp
from jax import lax
from jax.experimental import pallas as pl
from jax.experimental.pallas import tpu as pltpu
from jax.sharding import PartitionSpec as P

HEADS = 8
BLK = 128
EPS = 1e-06
LOG2E = 1.4426950408889634
OFF = -1e30
FLOOR = -1e20
MESH = pl.DeviceIdType.MESH
F32 = jnp.float32
BF16 = jnp.bfloat16
CORE, XX, YY, HALO, ZZ = range(5)


def flip(me, apart):
    wide = 1 << apart
    return me + wide - 2 * wide * ((me // wide) % 2)


def dot(a, b, over):
    return lax.dot_general(a, b, ((over[0], over[1]), ((), ())), preferred_element_type=F32)


def attend_kernel(
    peers, swaps,
    f_hbm, wq_hbm, wk_hbm, wv_hbm, lb_hbm, lc_hbm, eb_hbm, ec_hbm,
    ctx_ref,
    own, wq, wk, wv, lb, lc, eb, ec,
    kv, g, wvt, vt, bias, top, acc, raw,
    local_sem, send_sem, recv_sem, ready_sem,
):
    me = lax.axis_index("dom")
    odd = me % 2
    rows = own.shape[0]
    width = own.shape[1]
    head = width // HEADS
    beside = lax.rem(me + 2 * odd - 1 + peers, peers)
    partner = [flip(me, swaps[0]), flip(me, swaps[1]), flip(me, swaps[2]), beside, flip(me, swaps[3])]

    def waits(apart):
        low = 1 << apart
        usual = (me // low) % 2
        return jnp.where(me == 0, 1, jnp.where(me == low, 0, usual))

    even_end = me + odd
    late = [
        1 - odd,
        waits(swaps[1]),
        waits(swaps[2]),
        jnp.where(even_end % 8 == 0, odd, 1 - odd),
        waits(swaps[3]),
    ]

    barrier = pltpu.get_barrier_semaphore()
    for k in (ZZ, YY, XX, CORE, HALO):
        @pl.when(late[k] == 0)
        def _(k=k):
            pl.semaphore_signal(barrier, inc=1, device_id=(partner[k],), device_id_type=MESH)

    pulls = [
        pltpu.make_async_copy(src, dst, local_sem.at[i])
        for i, (src, dst) in enumerate(
            ((f_hbm, own), (wq_hbm, wq), (wk_hbm, wk), (wv_hbm, wv),
             (lb_hbm, lb), (lc_hbm, lc), (eb_hbm, eb), (ec_hbm, ec))
        )
    ]
    for pull in pulls:
        pull.start()

    def copies(k):
        if k == HALO:
            src = f_hbm.at[pl.ds(pl.multiple_of(odd * BLK, BLK), BLK)]
            dst = kv.at[k, pl.ds(0, BLK)]
        else:
            src, dst = f_hbm, kv.at[k]
        return pltpu.make_async_remote_copy(
            src_ref=src, dst_ref=dst, send_sem=send_sem.at[k], recv_sem=recv_sem.at[k],
            device_id=(partner[k],), device_id_type=MESH,
        )

    moves = [copies(k) for k in range(5)]
    greeted = late[0] + late[1] + late[2] + late[3] + late[4]

    @pl.when(greeted > 0)
    def _():
        pl.semaphore_wait(barrier, greeted)

    for k in (ZZ, YY, XX, CORE, HALO):
        @pl.when(late[k] == 1)
        def _(k=k):
            pl.semaphore_signal(ready_sem.at[k], inc=1, device_id=(partner[k],), device_id_type=MESH)
            moves[k].start()

    for i in range(4):
        pulls[i].wait()
    own_rows = own[...]
    scale = LOG2E * float(head) ** (-0.5)
    qt = (dot(wq[...], own_rows, ((0,), (1,))) * scale).astype(BF16)
    wvt[...] = wv[...].T
    for h in range(HEADS):
        parts = [qt[h * head:(h + 1) * head]]
        if h:
            parts.insert(0, jnp.zeros((h * head, rows), BF16))
        if h < HEADS - 1:
            parts.append(jnp.zeros((width - (h + 1) * head, rows), BF16))
        g[h] = dot(wk[...], jnp.concatenate(parts, axis=0), ((1,), (0,))).astype(BF16)

    for k in (CORE, HALO, XX, YY, ZZ):
        @pl.when(late[k] == 0)
        def _(k=k):
            pl.semaphore_wait(ready_sem.at[k], 1)
            moves[k].start()

    for i in range(4, 8):
        pulls[i].wait()

    def put(slot, block, counts):
        row = [
            jnp.full((1, BLK), jnp.where(c == 0, OFF, jnp.where(c == 1, 0.0, 1.0)).astype(F32))
            for c in counts
        ]
        bias[slot, pl.ds(block, 1), :] = jnp.concatenate(row, axis=1)

    def in_local(q, position):
        used = jnp.int32(0)
        for j in range(4):
            used += jnp.where((lb[q, j] == position) & (j < lc[q]), 1, 0)
        return used

    def in_match(m, q, block):
        used = jnp.int32(0)
        for j in range(2):
            used += jnp.where((eb[q, j, m] == block) & (j < ec[q, m]), 1, 0)
        return used

    near = [[in_local(q, j) for j in range(4)] for q in range(2)]
    for b in range(2):
        put(0, b, [near[q][1 + b] for q in range(2)])
        extra = [jnp.where(odd == b, near[q][0] if b else near[q][3], 0) for q in range(2)]
        put(1 + CORE, b, [in_match(0, q, b) + extra[q] for q in range(2)])
        for m, k in ((1, XX), (2, YY), (3, ZZ)):
            put(1 + k, b, [in_match(m, q, b) for q in range(2)])
    put(1 + HALO, 0, [jnp.where(odd == 1, near[q][3], near[q][0]) for q in range(2)])
    put(1 + HALO, 1, [jnp.int32(0)] * 2)

    kv[HALO, pl.ds(BLK, BLK), :] = jnp.zeros((BLK, width), BF16)
    for h in range(HEADS):
        vt[h, pl.ds(head, 16), :] = jnp.ones((16, rows), BF16)
    top[...] = jnp.full(top.shape, FLOOR, F32)
    acc[...] = jnp.zeros(acc.shape, F32)

    def part(keys, slot):
        values = dot(wvt[...], keys, ((1,), (1,))).astype(BF16)
        for h in range(HEADS):
            vt[h, pl.ds(0, head), :] = values[h * head:(h + 1) * head]
        for h in range(HEADS):
            raw[h] = dot(keys, g[h], ((1,), (0,)))
        for h in range(HEADS):
            scores = raw[h]
            first = bias[slot, pl.ds(0, 1), :]
            second = bias[slot, pl.ds(1, 1), :]
            old = top[h]
            new = jnp.maximum(
                old,
                jnp.maximum(
                    jnp.max(scores[:BLK], axis=0, keepdims=True) + first,
                    jnp.max(scores[BLK:], axis=0, keepdims=True) + second,
                ),
            )
            top[h] = new
            weights = jnp.concatenate(
                [
                    jnp.exp2(scores[:BLK] - (new - first)).astype(BF16),
                    jnp.exp2(scores[BLK:] - (new - second)).astype(BF16),
                ],
                axis=0,
            )
            out = dot(vt[h], weights, ((1,), (0,)))
            acc[h] = acc[h] * jnp.exp2(old - new) + out[: head + 8]

    part(own_rows, 0)

    for k in range(5):
        moves[k].wait_recv()
        part(kv[k], k + 1)

    for h in range(HEADS):
        ctx_ref[pl.ds(h * head, head), :] = (
            acc[h, pl.ds(0, head), :] / acc[h, pl.ds(head, 1), :]
        ).astype(BF16)
    for k in range(5):
        moves[k].wait_send()


def finish_kernel(ctx_ref, f_ref, w_ref, o_ref):
    mixed = dot(ctx_ref[...], w_ref[...], ((0,), (0,)))
    mean = jnp.mean(mixed * mixed, axis=-1, keepdims=True)
    o_ref[...] = (f_ref[...].astype(F32) + mixed * lax.rsqrt(mean + EPS)).astype(BF16)


def shards(features, w_query, w_key, w_value, w_out, local_blocks, local_count, expander_blocks, expander_count):
    rows, width = features.shape
    head = width // HEADS
    peers = lax.axis_size("dom")
    levels = peers.bit_length() - 1
    matches = expander_blocks.shape[0]
    swaps = [m * levels // matches for m in range(matches)]
    whole = pl.BlockSpec(memory_space=pltpu.HBM)
    inside = pl.BlockSpec(memory_space=pltpu.VMEM)
    expander_blocks = jnp.transpose(expander_blocks, (1, 2, 0))
    expander_count = expander_count.T
    ctx = pl.pallas_call(
        functools.partial(attend_kernel, peers, swaps),
        out_shape=jax.ShapeDtypeStruct((width, rows), BF16),
        in_specs=[whole] * 8,
        out_specs=inside,
        scratch_shapes=[
            pltpu.VMEM((rows, width), BF16),
            pltpu.VMEM((width, width), BF16),
            pltpu.VMEM((width, width), BF16),
            pltpu.VMEM((width, width), BF16),
            pltpu.SMEM(local_blocks.shape, jnp.int32),
            pltpu.SMEM(local_count.shape, jnp.int32),
            pltpu.SMEM(expander_blocks.shape, jnp.int32),
            pltpu.SMEM(expander_count.shape, jnp.int32),
            pltpu.VMEM((5, rows, width), BF16),
            pltpu.VMEM((HEADS, width, rows), BF16),
            pltpu.VMEM((width, width), BF16),
            pltpu.VMEM((HEADS, head + 16, rows), BF16),
            pltpu.VMEM((6, 8, rows), F32),
            pltpu.VMEM((HEADS, 1, rows), F32),
            pltpu.VMEM((HEADS, head + 8, rows), F32),
            pltpu.VMEM((HEADS, rows, rows), F32),
            pltpu.SemaphoreType.DMA((8,)),
            pltpu.SemaphoreType.DMA((5,)),
            pltpu.SemaphoreType.DMA((5,)),
            pltpu.SemaphoreType.REGULAR((5,)),
        ],
        compiler_params=pltpu.CompilerParams(
            collective_id=0, has_side_effects=True, vmem_limit_bytes=32 << 20
        ),
        name="attend",
    )(*[pltpu.with_memory_space_constraint(a, pltpu.HBM) for a in (features, w_query, w_key, w_value, local_blocks, local_count, expander_blocks, expander_count)])
    return pl.pallas_call(
        finish_kernel,
        out_shape=jax.ShapeDtypeStruct((rows, width), BF16),
        in_specs=[inside] * 3,
        out_specs=inside,
        compiler_params=pltpu.CompilerParams(vmem_limit_bytes=8 << 20),
        name="finish",
    )(ctx, features, w_out)


def solution(mesh):
    in_specs = (
        P("dom", None), P(), P(), P(), P(),
        P("dom", None), P("dom"), P(None, "dom", None), P(None, "dom"),
    )
    return jax.shard_map(
        shards, mesh=mesh, in_specs=in_specs, out_specs=P("dom", None), check_vma=False
    )
```

```python
import functools

import jax
import jax.numpy as jnp
from jax import lax
from jax.experimental import pallas as pl
from jax.experimental.pallas import tpu as pltpu
from jax.sharding import PartitionSpec as P

HEADS = 8
BLK = 128
EPS = 1e-06
LOG2E = 1.4426950408889634
OFF = -1e30
FLOOR = -1e20
MESH = pl.DeviceIdType.MESH
F32 = jnp.float32
BF16 = jnp.bfloat16
CORE, XX, YY, HALO, ZZ = range(5)
MOVES = 6


def flip(me, apart):
    wide = 1 << apart
    return me + wide - 2 * wide * ((me // wide) % 2)


def dot(a, b, over):
    return lax.dot_general(a, b, ((over[0], over[1]), ((), ())), preferred_element_type=F32)


def attend_kernel(
    peers, swaps,
    f_hbm, wq_hbm, wk_hbm, wv_hbm, lb_hbm, lc_hbm, eb_hbm, ec_hbm,
    ctx_ref,
    own, wq, wk, wv, lb, lc, eb, ec,
    kv, g, wvt, vt, bias, top, acc, raw,
    local_sem, send_sem, recv_sem, ok_sem, ready_sem,
):
    me = lax.axis_index("dom")
    odd = me % 2
    rows = own.shape[0]
    width = own.shape[1]
    head = width // HEADS
    beside = lax.rem(me + 2 * odd - 1 + peers, peers)
    far = {XX: 1 << swaps[1], YY: 1 << swaps[2], ZZ: 1 << swaps[3]}
    partner = {
        CORE: flip(me, swaps[0]), XX: flip(me, swaps[1]), YY: flip(me, swaps[2]),
        HALO: beside, ZZ: flip(me, swaps[3]),
    }

    cut = 3 * peers // 4
    late_halo = (me == peers - 1) | (me == cut - 1)
    even = odd == 0
    bit = {k: (me // far[k]) % 2 for k in (XX, YY, ZZ)}
    upper = bit[ZZ] == 1
    plane = 2 * far[YY]
    beyond = me >= peers // 2

    def precedes(who, by):
        return (who % plane == plane - by) & (upper | beyond)

    apart = precedes(me, 1)
    stands_in = precedes(me, 2)
    late = {k: (me == 0) | ((bit[k] == 1) & (me != far[k])) for k in (XX, YY)}
    barrier = pltpu.get_barrier_semaphore()

    def greet(who):
        pl.semaphore_signal(barrier, inc=1, device_id=(who,), device_id_type=MESH)

    def tell(sem, who):
        pl.semaphore_signal(sem, inc=1, device_id=(who,), device_id_type=MESH)

    @pl.when(me > 0)
    def _():
        q = partner[ZZ]
        greet(jnp.where(q == 1, 1, q - q % 2))
        greet(partner[CORE])
        for k in (YY, XX):
            @pl.when(jnp.logical_not(late[k]))
            def _(k=k):
                q = partner[k]
                r = q + 1 - q % 2
                greet(jnp.where(q == 0, 0, jnp.where(precedes(r, 1), r - 1, r)))

    @pl.when(jnp.logical_not(late_halo))
    def _():
        greet(jnp.where(precedes(me, 3), beside, beside + odd))

    pulls = [
        pltpu.make_async_copy(src, dst, local_sem.at[i])
        for i, (src, dst) in enumerate(
            ((f_hbm, own), (wq_hbm, wq), (wk_hbm, wk), (wv_hbm, wv),
             (lb_hbm, lb), (lc_hbm, lc), (eb_hbm, eb), (ec_hbm, ec))
        )
    ]
    for pull in pulls:
        pull.start()

    def move(i, src, dst, who):
        return pltpu.make_async_remote_copy(
            src_ref=src, dst_ref=dst, send_sem=send_sem.at[i], recv_sem=recv_sem.at[i],
            device_id=(who,), device_id_type=MESH,
        )

    top_half, low_half = pl.ds(0, BLK), pl.ds(BLK, BLK)
    shared = pl.ds(pl.multiple_of(odd * BLK, BLK), BLK)
    moves = [move(k, f_hbm, kv.at[k], partner[k]) for k in (CORE, XX, YY)] + [
        move(HALO, f_hbm.at[shared], kv.at[HALO, top_half], beside),
        move(ZZ, f_hbm.at[top_half], kv.at[ZZ, top_half], partner[ZZ]),
        move(ZZ + 1, f_hbm.at[low_half], kv.at[ZZ, low_half], partner[ZZ]),
    ]

    def send(k):
        moves[k].start()
        if k == ZZ:
            moves[ZZ + 1].start()

    def give_ready(mate):
        for k in (YY, XX):
            @pl.when(bit[k] == 1)
            def _(k=k):
                tell(ready_sem.at[k], partner[k])

                @pl.when(partner[k] + mate != 0)
                def _():
                    tell(ready_sem.at[k], partner[k] + mate)

    def send_late():
        for k in (YY, XX):
            @pl.when(late[k])
            def _(k=k):
                send(k)

    def even_hears():
        usual = jnp.where(stands_in, 8, 3)
        pl.semaphore_wait(barrier, jnp.where(me == 0, 4, jnp.where(me == far[ZZ], 2, usual)))

        @pl.when(me == 0)
        def _():
            for k in (ZZ, YY, XX, CORE):
                tell(ready_sem.at[k], partner[k])
            for k in (CORE, ZZ, YY, XX):
                send(k)

        @pl.when(me > 0)
        def _():
            tell(ok_sem, partner[CORE])

            @pl.when(me != far[ZZ])
            def _():
                send(ZZ)

            send(CORE)

        @pl.when(stands_in)
        def _():
            give_ready(1)
            send(HALO)
            send_late()

    def even_told():
        pl.semaphore_wait(ok_sem, 1)

        @pl.when(me != cut)
        def _():
            send(HALO)

        send_late()

    def odd_told():
        pl.semaphore_wait(ok_sem, 1)
        send(ZZ)

        @pl.when(apart)
        def _():
            send_late()

    def odd_hears():
        usual = 3 + 2 * bit[XX] + 2 * bit[YY]
        fewer = (me == far[XX] + 1) | (me == far[YY] + 1) | (me == cut + 1)
        count = jnp.where((me == 1) | apart, 2, jnp.where(fewer, usual - 1, usual))
        pl.semaphore_wait(barrier, count)

        @pl.when(late_halo)
        def _():
            tell(ready_sem.at[HALO], beside)

        @pl.when((me > 1) & jnp.logical_not(apart))
        def _():
            tell(ok_sem, partner[CORE])
            give_ready(-1)

        @pl.when(me == 1)
        def _():
            send(ZZ)

        send(HALO)

        @pl.when(me > 1)
        def _():
            send(CORE)

        @pl.when(jnp.logical_not(apart))
        def _():
            send_late()

    corner = me % plane <= 1
    even_z_first = upper | beyond | corner
    odd_z_first = (upper | corner) & (me > 1) & jnp.logical_not(apart)

    @pl.when(even & even_z_first)
    def _():
        even_hears()

    @pl.when((odd == 1) & odd_z_first)
    def _():
        odd_told()

    @pl.when((odd == 1) & jnp.logical_not(corner))
    def _():
        odd_hears()

    @pl.when(even & jnp.logical_not(corner | stands_in))
    def _():
        even_told()

    @pl.when(even & jnp.logical_not(even_z_first))
    def _():
        even_hears()

    @pl.when((odd == 1) & (beyond | apart) & jnp.logical_not(odd_z_first))
    def _():
        odd_told()

    for i in range(4):
        pulls[i].wait()
    own_rows = own[...]
    scale = LOG2E * float(head) ** (-0.5)
    qt = (dot(wq[...], own_rows, ((0,), (1,))) * scale).astype(BF16)
    wvt[...] = wv[...].T
    for h in range(HEADS):
        parts = [qt[h * head:(h + 1) * head]]
        if h:
            parts.insert(0, jnp.zeros((h * head, rows), BF16))
        if h < HEADS - 1:
            parts.append(jnp.zeros((width - (h + 1) * head, rows), BF16))
        g[h] = dot(wk[...], jnp.concatenate(parts, axis=0), ((1,), (0,))).astype(BF16)

    @pl.when((odd == 1) & corner)
    def _():
        odd_hears()

    @pl.when(even & corner & (me > 0))
    def _():
        even_told()

    for k in (XX, YY):
        @pl.when(jnp.logical_not(late[k]) & (me != far[k]))
        def _(k=k):
            pl.semaphore_wait(ready_sem.at[k], 1)
            send(k)

    @pl.when((odd == 1) & jnp.logical_not(beyond | apart | odd_z_first) & (me > 1))
    def _():
        odd_told()

    for i in range(4, 8):
        pulls[i].wait()

    def put(slot, block, counts):
        row = [
            jnp.full((1, BLK), jnp.where(c == 0, OFF, jnp.where(c == 1, 0.0, 1.0)).astype(F32))
            for c in counts
        ]
        bias[slot, pl.ds(block, 1), :] = jnp.concatenate(row, axis=1)

    def in_local(q, position):
        used = jnp.int32(0)
        for j in range(4):
            used += jnp.where((lb[q, j] == position) & (j < lc[q]), 1, 0)
        return used

    def in_match(m, q, block):
        used = jnp.int32(0)
        for j in range(2):
            used += jnp.where((eb[q, j, m] == block) & (j < ec[q, m]), 1, 0)
        return used

    near = [[in_local(q, j) for j in range(4)] for q in range(2)]
    for b in range(2):
        put(0, b, [near[q][1 + b] for q in range(2)])
        extra = [jnp.where(odd == b, near[q][0] if b else near[q][3], 0) for q in range(2)]
        put(1 + CORE, b, [in_match(0, q, b) + extra[q] for q in range(2)])
        for m, k in ((1, XX), (2, YY), (3, ZZ)):
            put(1 + k, b, [in_match(m, q, b) for q in range(2)])
    put(1 + HALO, 0, [jnp.where(odd == 1, near[q][3], near[q][0]) for q in range(2)])

    for h in range(HEADS):
        vt[h, pl.ds(head, 16), :] = jnp.ones((16, rows), BF16)
    top[...] = jnp.full(top.shape, FLOOR, F32)
    acc[...] = jnp.zeros(acc.shape, F32)

    def part(keys, slot, blocks):
        span = BLK * len(blocks)
        values = dot(wvt[...], keys, ((1,), (1,))).astype(BF16)
        for h in range(HEADS):
            vt[h, pl.ds(0, head), pl.ds(0, span)] = values[h * head:(h + 1) * head]
        for h in range(HEADS):
            raw[h, pl.ds(0, span)] = dot(keys, g[h], ((1,), (0,)))
        offsets = [bias[slot, pl.ds(b, 1), :] for b in blocks]
        for h in range(HEADS):
            scores = [raw[h, pl.ds(i * BLK, BLK)] for i in range(len(blocks))]
            old = top[h]
            new = old
            for score, offset in zip(scores, offsets):
                new = jnp.maximum(new, jnp.max(score, axis=0, keepdims=True) + offset)
            top[h] = new
            weights = [
                jnp.exp2(score - (new - offset)).astype(BF16)
                for score, offset in zip(scores, offsets)
            ]
            weights = jnp.concatenate(weights, axis=0) if len(blocks) > 1 else weights[0]
            out = dot(vt[h, :, pl.ds(0, span)], weights, ((1,), (0,)))
            acc[h] = acc[h] * jnp.exp2(old - new) + out[: head + 8]

    part(own_rows, 0, (0, 1))

    def answer(who, k):
        @pl.when(me == who)
        def _():
            pl.semaphore_wait(ready_sem.at[k], 1)
            send(k)

    for who, k in ((1, CORE), (far[XX], XX), (far[YY], YY), (far[ZZ], ZZ), (cut, HALO)):
        answer(who, k)

    def full(k):
        move(k, f_hbm, kv.at[k], partner[CORE]).wait_recv()
        part(kv[k], k + 1, (0, 1))

    def halo():
        moves[HALO].wait_recv()
        part(kv[HALO, top_half], 1 + HALO, (0,))

    def half(b):
        moves[ZZ + b].wait_recv()
        part(kv[ZZ, (top_half, low_half)[b]], 1 + ZZ, (b,))

    wraps = (me % plane == 0) | (me % plane == 2) | (me % plane == plane - 1)
    inner = (me // plane) % 2 != bit[ZZ]

    @pl.when(me != 1)
    def _():
        full(CORE)

    @pl.when(jnp.logical_not(wraps))
    def _():
        halo()

    @pl.when(inner)
    def _():
        half(0)
        half(1)

    @pl.when(jnp.logical_not(corner))
    def _():
        full(YY)

    @pl.when(jnp.logical_not(inner))
    def _():
        half(0)

    full(XX)

    @pl.when(jnp.logical_not(inner))
    def _():
        half(1)

    @pl.when(corner)
    def _():
        full(YY)

    @pl.when(me == 1)
    def _():
        full(CORE)

    answer(0, HALO)

    @pl.when(wraps)
    def _():
        halo()

    for h in range(HEADS):
        ctx_ref[pl.ds(h * head, head), :] = (
            acc[h, pl.ds(0, head), :] / acc[h, pl.ds(head, 1), :]
        ).astype(BF16)
    for i in range(MOVES):
        moves[i].wait_send()


def finish_kernel(ctx_ref, f_ref, w_ref, o_ref):
    mixed = dot(ctx_ref[...], w_ref[...], ((0,), (0,)))
    mean = jnp.mean(mixed * mixed, axis=-1, keepdims=True)
    o_ref[...] = (f_ref[...].astype(F32) + mixed * lax.rsqrt(mean + EPS)).astype(BF16)


def shards(features, w_query, w_key, w_value, w_out, local_blocks, local_count, expander_blocks, expander_count):
    rows, width = features.shape
    head = width // HEADS
    peers = lax.axis_size("dom")
    levels = peers.bit_length() - 1
    matches = expander_blocks.shape[0]
    swaps = [m * levels // matches for m in range(matches)]
    whole = pl.BlockSpec(memory_space=pltpu.HBM)
    inside = pl.BlockSpec(memory_space=pltpu.VMEM)
    expander_blocks = jnp.transpose(expander_blocks, (1, 2, 0))
    expander_count = expander_count.T
    ctx = pl.pallas_call(
        functools.partial(attend_kernel, peers, swaps),
        out_shape=jax.ShapeDtypeStruct((width, rows), BF16),
        in_specs=[whole] * 8,
        out_specs=inside,
        scratch_shapes=[
            pltpu.VMEM((rows, width), BF16),
            pltpu.VMEM((width, width), BF16),
            pltpu.VMEM((width, width), BF16),
            pltpu.VMEM((width, width), BF16),
            pltpu.SMEM(local_blocks.shape, jnp.int32),
            pltpu.SMEM(local_count.shape, jnp.int32),
            pltpu.SMEM(expander_blocks.shape, jnp.int32),
            pltpu.SMEM(expander_count.shape, jnp.int32),
            pltpu.VMEM((5, rows, width), BF16),
            pltpu.VMEM((HEADS, width, rows), BF16),
            pltpu.VMEM((width, width), BF16),
            pltpu.VMEM((HEADS, head + 16, rows), BF16),
            pltpu.VMEM((6, 8, rows), F32),
            pltpu.VMEM((HEADS, 1, rows), F32),
            pltpu.VMEM((HEADS, head + 8, rows), F32),
            pltpu.VMEM((HEADS, rows, rows), F32),
            pltpu.SemaphoreType.DMA((8,)),
            pltpu.SemaphoreType.DMA((MOVES,)),
            pltpu.SemaphoreType.DMA((MOVES,)),
            pltpu.SemaphoreType.REGULAR,
            pltpu.SemaphoreType.REGULAR((5,)),
        ],
        compiler_params=pltpu.CompilerParams(
            collective_id=0, has_side_effects=True, vmem_limit_bytes=32 << 20
        ),
        name="attend",
    )(*[pltpu.with_memory_space_constraint(a, pltpu.HBM) for a in (features, w_query, w_key, w_value, local_blocks, local_count, expander_blocks, expander_count)])
    return pl.pallas_call(
        finish_kernel,
        out_shape=jax.ShapeDtypeStruct((rows, width), BF16),
        in_specs=[inside] * 3,
        out_specs=inside,
        compiler_params=pltpu.CompilerParams(vmem_limit_bytes=8 << 20),
        name="finish",
    )(ctx, features, w_out)


def solution(mesh):
    in_specs = (
        P("dom", None), P(), P(), P(), P(),
        P("dom", None), P("dom"), P(None, "dom", None), P(None, "dom"),
    )
    return jax.shard_map(
        shards, mesh=mesh, in_specs=in_specs, out_specs=P("dom", None), check_vma=False
    )
```

```python
import functools

import jax
import jax.numpy as jnp
from jax import lax
from jax.experimental import pallas as pl
from jax.experimental.pallas import tpu as pltpu
from jax.sharding import PartitionSpec as P

HEADS = 8
BLK = 128
EPS = 1e-06
LOG2E = 1.4426950408889634
OFF = -1e30
FLOOR = -1e20
MESH = pl.DeviceIdType.MESH
F32 = jnp.float32
BF16 = jnp.bfloat16
CORE, XX, YY, HALO, ZZ = range(5)
MOVES = 6


def flip(me, apart):
    wide = 1 << apart
    return me + wide - 2 * wide * ((me // wide) % 2)


def dot(a, b, over):
    return lax.dot_general(a, b, ((over[0], over[1]), ((), ())), preferred_element_type=F32)


def attend_kernel(
    peers, swaps,
    f_hbm, wq_hbm, wk_hbm, wv_hbm, lb_hbm, lc_hbm, eb_hbm, ec_hbm,
    ctx_ref,
    own, wq, wk, wv, lb, lc, eb, ec,
    kv, g, wvt, vt, bias, top, acc, raw,
    local_sem, send_sem, recv_sem, ok_sem, ready_sem,
):
    me = lax.axis_index("dom")
    odd = me % 2
    rows = own.shape[0]
    width = own.shape[1]
    head = width // HEADS
    beside = lax.rem(me + 2 * odd - 1 + peers, peers)
    far = {XX: 1 << swaps[1], YY: 1 << swaps[2], ZZ: 1 << swaps[3]}
    partner = {
        CORE: flip(me, swaps[0]), XX: flip(me, swaps[1]), YY: flip(me, swaps[2]),
        HALO: beside, ZZ: flip(me, swaps[3]),
    }

    cut = 3 * peers // 4
    late_halo = (me == peers - 1) | (me == cut - 1)
    even = odd == 0
    bit = {k: (me // far[k]) % 2 for k in (XX, YY, ZZ)}
    upper = bit[ZZ] == 1
    plane = 2 * far[YY]
    beyond = me >= peers // 2

    def precedes(who, by):
        return (who % plane == plane - by) & ((upper & ((me // plane) % 2 == 1)) | beyond)

    apart = precedes(me, 1)
    stands_in = precedes(me, 2)
    late = {k: (me == 0) | ((bit[k] == 1) & (me != far[k])) for k in (XX, YY)}
    barrier = pltpu.get_barrier_semaphore()

    def greet(who):
        pl.semaphore_signal(barrier, inc=1, device_id=(who,), device_id_type=MESH)

    def tell(sem, who):
        pl.semaphore_signal(sem, inc=1, device_id=(who,), device_id_type=MESH)

    @pl.when(me > 0)
    def _():
        q = partner[ZZ]
        greet(jnp.where(q == 1, 1, q - q % 2))
        greet(partner[CORE])
        for k in (YY, XX):
            @pl.when(jnp.logical_not(late[k]))
            def _(k=k):
                q = partner[k]
                r = q + 1 - q % 2
                greet(jnp.where(q == 0, 0, jnp.where(precedes(r, 1), r - 1, r)))

    @pl.when(jnp.logical_not(late_halo))
    def _():
        greet(jnp.where(precedes(me, 3), beside, beside + odd))

    pulls = [
        pltpu.make_async_copy(src, dst, local_sem.at[i])
        for i, (src, dst) in enumerate(
            ((f_hbm, own), (wq_hbm, wq), (wk_hbm, wk), (wv_hbm, wv),
             (lb_hbm, lb), (lc_hbm, lc), (eb_hbm, eb), (ec_hbm, ec))
        )
    ]
    for pull in pulls:
        pull.start()

    def move(i, src, dst, who):
        return pltpu.make_async_remote_copy(
            src_ref=src, dst_ref=dst, send_sem=send_sem.at[i], recv_sem=recv_sem.at[i],
            device_id=(who,), device_id_type=MESH,
        )

    top_half, low_half = pl.ds(0, BLK), pl.ds(BLK, BLK)
    shared = pl.ds(pl.multiple_of(odd * BLK, BLK), BLK)
    moves = [move(k, f_hbm, kv.at[k], partner[k]) for k in (CORE, XX, YY)] + [
        move(HALO, f_hbm.at[shared], kv.at[HALO, top_half], beside),
        move(ZZ, f_hbm.at[top_half], kv.at[ZZ, top_half], partner[ZZ]),
        move(ZZ + 1, f_hbm.at[low_half], kv.at[ZZ, low_half], partner[ZZ]),
    ]

    def send(k):
        moves[k].start()
        if k == ZZ:
            moves[ZZ + 1].start()

    def give_ready(mate):
        for k in (YY, XX):
            @pl.when(bit[k] == 1)
            def _(k=k):
                tell(ready_sem.at[k], partner[k])

                @pl.when(partner[k] + mate != 0)
                def _():
                    tell(ready_sem.at[k], partner[k] + mate)

    def send_late():
        for k in (YY, XX):
            @pl.when(late[k])
            def _(k=k):
                send(k)

    def even_hears():
        usual = jnp.where(stands_in, 8, 3)
        pl.semaphore_wait(barrier, jnp.where(me == 0, 4, jnp.where(me == far[ZZ], 2, usual)))

        @pl.when(me == 0)
        def _():
            for k in (ZZ, YY, XX, CORE):
                tell(ready_sem.at[k], partner[k])
            for k in (CORE, ZZ, YY, XX):
                send(k)

        @pl.when(me > 0)
        def _():
            tell(ok_sem, partner[CORE])

            @pl.when(me != far[ZZ])
            def _():
                send(ZZ)

            send(CORE)

        @pl.when(stands_in)
        def _():
            give_ready(1)
            send(HALO)
            send_late()

    def even_told():
        pl.semaphore_wait(ok_sem, 1)

        @pl.when(me != cut)
        def _():
            send(HALO)

        send_late()

    def odd_told():
        pl.semaphore_wait(ok_sem, 1)
        send(ZZ)

        @pl.when(apart)
        def _():
            send_late()

    def odd_hears():
        usual = 3 + 2 * bit[XX] + 2 * bit[YY]
        fewer = (me == far[XX] + 1) | (me == far[YY] + 1) | (me == cut + 1)
        count = jnp.where((me == 1) | apart, 2, jnp.where(fewer, usual - 1, usual))
        pl.semaphore_wait(barrier, count)

        @pl.when(late_halo)
        def _():
            tell(ready_sem.at[HALO], beside)

        @pl.when((me > 1) & jnp.logical_not(apart))
        def _():
            tell(ok_sem, partner[CORE])
            give_ready(-1)

        @pl.when(me == 1)
        def _():
            send(ZZ)

        send(HALO)

        @pl.when(me > 1)
        def _():
            send(CORE)

        @pl.when(jnp.logical_not(apart))
        def _():
            send_late()

    corner = me % plane <= 1
    even_z_first = upper | beyond | corner
    odd_z_first = (upper | corner) & (me > 1) & jnp.logical_not(apart)

    @pl.when(even & even_z_first)
    def _():
        even_hears()

    @pl.when((odd == 1) & odd_z_first)
    def _():
        odd_told()

    @pl.when((odd == 1) & jnp.logical_not(corner))
    def _():
        odd_hears()

    @pl.when(even & jnp.logical_not(corner | stands_in))
    def _():
        even_told()

    @pl.when(even & jnp.logical_not(even_z_first))
    def _():
        even_hears()

    @pl.when((odd == 1) & (beyond | apart) & jnp.logical_not(odd_z_first))
    def _():
        odd_told()

    for i in range(4):
        pulls[i].wait()
    own_rows = own[...]
    scale = LOG2E * float(head) ** (-0.5)
    qt = (dot(wq[...], own_rows, ((0,), (1,))) * scale).astype(BF16)
    wvt[...] = wv[...].T
    for h in range(HEADS):
        parts = [qt[h * head:(h + 1) * head]]
        if h:
            parts.insert(0, jnp.zeros((h * head, rows), BF16))
        if h < HEADS - 1:
            parts.append(jnp.zeros((width - (h + 1) * head, rows), BF16))
        g[h] = dot(wk[...], jnp.concatenate(parts, axis=0), ((1,), (0,))).astype(BF16)

    @pl.when((odd == 1) & corner)
    def _():
        odd_hears()

    @pl.when(even & corner & (me > 0))
    def _():
        even_told()

    for k in (XX, YY):
        @pl.when(jnp.logical_not(late[k]) & (me != far[k]))
        def _(k=k):
            pl.semaphore_wait(ready_sem.at[k], 1)
            send(k)

    @pl.when((odd == 1) & jnp.logical_not(beyond | apart | odd_z_first) & (me > 1))
    def _():
        odd_told()

    for i in range(4, 8):
        pulls[i].wait()

    def put(slot, block, counts):
        row = [
            jnp.full((1, BLK), jnp.where(c == 0, OFF, jnp.where(c == 1, 0.0, 1.0)).astype(F32))
            for c in counts
        ]
        bias[slot, pl.ds(block, 1), :] = jnp.concatenate(row, axis=1)

    def in_local(q, position):
        used = jnp.int32(0)
        for j in range(4):
            used += jnp.where((lb[q, j] == position) & (j < lc[q]), 1, 0)
        return used

    def in_match(m, q, block):
        used = jnp.int32(0)
        for j in range(2):
            used += jnp.where((eb[q, j, m] == block) & (j < ec[q, m]), 1, 0)
        return used

    near = [[in_local(q, j) for j in range(4)] for q in range(2)]
    for b in range(2):
        put(0, b, [near[q][1 + b] for q in range(2)])
        extra = [jnp.where(odd == b, near[q][0] if b else near[q][3], 0) for q in range(2)]
        put(1 + CORE, b, [in_match(0, q, b) + extra[q] for q in range(2)])
        for m, k in ((1, XX), (2, YY), (3, ZZ)):
            put(1 + k, b, [in_match(m, q, b) for q in range(2)])
    put(1 + HALO, 0, [jnp.where(odd == 1, near[q][3], near[q][0]) for q in range(2)])

    for h in range(HEADS):
        vt[h, pl.ds(head, 16), :] = jnp.ones((16, rows), BF16)
    top[...] = jnp.full(top.shape, FLOOR, F32)
    acc[...] = jnp.zeros(acc.shape, F32)

    def part(keys, slot, blocks):
        span = BLK * len(blocks)
        values = dot(wvt[...], keys, ((1,), (1,))).astype(BF16)
        for h in range(HEADS):
            vt[h, pl.ds(0, head), pl.ds(0, span)] = values[h * head:(h + 1) * head]
        for h in range(HEADS):
            raw[h, pl.ds(0, span)] = dot(keys, g[h], ((1,), (0,)))
        offsets = [bias[slot, pl.ds(b, 1), :] for b in blocks]
        for h in range(HEADS):
            scores = [raw[h, pl.ds(i * BLK, BLK)] for i in range(len(blocks))]
            old = top[h]
            new = old
            for score, offset in zip(scores, offsets):
                new = jnp.maximum(new, jnp.max(score, axis=0, keepdims=True) + offset)
            top[h] = new
            weights = [
                jnp.exp2(score - (new - offset)).astype(BF16)
                for score, offset in zip(scores, offsets)
            ]
            weights = jnp.concatenate(weights, axis=0) if len(blocks) > 1 else weights[0]
            out = dot(vt[h, :, pl.ds(0, span)], weights, ((1,), (0,)))
            acc[h] = acc[h] * jnp.exp2(old - new) + out[: head + 8]

    part(own_rows, 0, (0, 1))

    def answer(who, k):
        @pl.when(me == who)
        def _():
            pl.semaphore_wait(ready_sem.at[k], 1)
            send(k)

    for who, k in ((1, CORE), (far[XX], XX), (far[YY], YY), (far[ZZ], ZZ), (cut, HALO)):
        answer(who, k)

    def full(k):
        move(k, f_hbm, kv.at[k], partner[CORE]).wait_recv()
        part(kv[k], k + 1, (0, 1))

    def halo():
        moves[HALO].wait_recv()
        part(kv[HALO, top_half], 1 + HALO, (0,))

    def half(b):
        moves[ZZ + b].wait_recv()
        part(kv[ZZ, (top_half, low_half)[b]], 1 + ZZ, (b,))

    wraps = (me % plane == 0) | (me % plane == 2) | (me % plane == plane - 1)
    inner = (me // plane) % 2 != bit[ZZ]

    @pl.when(me != 1)
    def _():
        full(CORE)

    @pl.when(jnp.logical_not(wraps))
    def _():
        halo()

    @pl.when(inner)
    def _():
        half(0)
        half(1)

    edge = me % (2 * far[XX]) <= 1

    @pl.when(edge & jnp.logical_not(inner))
    def _():
        half(0)

    @pl.when(jnp.logical_not(corner))
    def _():
        full(YY)

    @pl.when(jnp.logical_not(edge | inner))
    def _():
        half(0)

    full(XX)

    @pl.when(jnp.logical_not(inner))
    def _():
        half(1)

    @pl.when(corner)
    def _():
        full(YY)

    @pl.when(me == 1)
    def _():
        full(CORE)

    answer(0, HALO)

    @pl.when(wraps)
    def _():
        halo()

    for h in range(HEADS):
        share = 1.0 / acc[h, pl.ds(head, 1), :]
        ctx_ref[pl.ds(h * head, head), :] = (acc[h, pl.ds(0, head), :] * share).astype(BF16)
    for i in range(MOVES):
        moves[i].wait_send()


def finish_kernel(ctx_ref, f_ref, w_ref, o_hbm, done, sem):
    rows = f_ref.shape[0]
    copies = []
    for b in range(rows // BLK):
        block = pl.ds(b * BLK, BLK)
        mixed = dot(ctx_ref[:, block], w_ref[...], ((0,), (0,)))
        mean = jnp.mean(mixed * mixed, axis=-1, keepdims=True)
        done[block, :] = (f_ref[block, :].astype(F32) + mixed * lax.rsqrt(mean + EPS)).astype(BF16)
        copies.append(pltpu.make_async_copy(done.at[block], o_hbm.at[block], sem.at[b]))
        copies[-1].start()
    for copy in copies:
        copy.wait()


def shards(features, w_query, w_key, w_value, w_out, local_blocks, local_count, expander_blocks, expander_count):
    rows, width = features.shape
    head = width // HEADS
    peers = lax.axis_size("dom")
    levels = peers.bit_length() - 1
    matches = expander_blocks.shape[0]
    swaps = [m * levels // matches for m in range(matches)]
    whole = pl.BlockSpec(memory_space=pltpu.HBM)
    inside = pl.BlockSpec(memory_space=pltpu.VMEM)
    expander_blocks = jnp.transpose(expander_blocks, (1, 2, 0))
    expander_count = expander_count.T
    ctx = pl.pallas_call(
        functools.partial(attend_kernel, peers, swaps),
        out_shape=jax.ShapeDtypeStruct((width, rows), BF16),
        in_specs=[whole] * 8,
        out_specs=inside,
        scratch_shapes=[
            pltpu.VMEM((rows, width), BF16),
            pltpu.VMEM((width, width), BF16),
            pltpu.VMEM((width, width), BF16),
            pltpu.VMEM((width, width), BF16),
            pltpu.SMEM(local_blocks.shape, jnp.int32),
            pltpu.SMEM(local_count.shape, jnp.int32),
            pltpu.SMEM(expander_blocks.shape, jnp.int32),
            pltpu.SMEM(expander_count.shape, jnp.int32),
            pltpu.VMEM((5, rows, width), BF16),
            pltpu.VMEM((HEADS, width, rows), BF16),
            pltpu.VMEM((width, width), BF16),
            pltpu.VMEM((HEADS, head + 16, rows), BF16),
            pltpu.VMEM((6, 8, rows), F32),
            pltpu.VMEM((HEADS, 1, rows), F32),
            pltpu.VMEM((HEADS, head + 8, rows), F32),
            pltpu.VMEM((HEADS, rows, rows), F32),
            pltpu.SemaphoreType.DMA((8,)),
            pltpu.SemaphoreType.DMA((MOVES,)),
            pltpu.SemaphoreType.DMA((MOVES,)),
            pltpu.SemaphoreType.REGULAR,
            pltpu.SemaphoreType.REGULAR((5,)),
        ],
        compiler_params=pltpu.CompilerParams(
            collective_id=0, has_side_effects=True, vmem_limit_bytes=32 << 20
        ),
        name="attend",
    )(*[pltpu.with_memory_space_constraint(a, pltpu.HBM) for a in (features, w_query, w_key, w_value, local_blocks, local_count, expander_blocks, expander_count)])
    return pl.pallas_call(
        finish_kernel,
        out_shape=jax.ShapeDtypeStruct((rows, width), BF16),
        in_specs=[inside] * 3,
        out_specs=whole,
        scratch_shapes=[pltpu.VMEM((rows, width), BF16), pltpu.SemaphoreType.DMA((rows // BLK,))],
        compiler_params=pltpu.CompilerParams(vmem_limit_bytes=8 << 20),
        name="finish",
    )(ctx, features, w_out)


def solution(mesh):
    in_specs = (
        P("dom", None), P(), P(), P(), P(),
        P("dom", None), P("dom"), P(None, "dom", None), P(None, "dom"),
    )
    return jax.shard_map(
        shards, mesh=mesh, in_specs=in_specs, out_specs=P("dom", None), check_vma=False
    )
```

```python
import functools

import jax
import jax.numpy as jnp
from jax import lax
from jax.experimental import pallas as pl
from jax.experimental.pallas import tpu as pltpu
from jax.sharding import PartitionSpec as P

HEADS = 8
BLK = 128
EPS = 1e-06
LOG2E = 1.4426950408889634
OFF = -1e30
FLOOR = -1e20
MESH = pl.DeviceIdType.MESH
F32 = jnp.float32
BF16 = jnp.bfloat16
CORE, XX, YY, HALO, ZZ = range(5)
MOVES = 6


def rem(a, b):
    return lax.rem(a, jnp.int32(b))


def div(a, b):
    return lax.div(a, jnp.int32(b))


def flip(me, apart):
    wide = 1 << apart
    return me + wide - 2 * wide * rem(div(me, wide), 2)


def dot(a, b, over):
    return lax.dot_general(a, b, ((over[0], over[1]), ((), ())), preferred_element_type=F32)


def attend_kernel(
    peers, swaps,
    f_hbm, wq_hbm, wk_hbm, wv_hbm, lb_hbm, lc_hbm, eb_hbm, ec_hbm,
    ctx_ref,
    own, wq, wk, wv, lb, lc, eb, ec,
    kv, g, wvt, vt, bias, top, acc, raw,
    local_sem, send_sem, recv_sem, ok_sem, ready_sem,
):
    me = lax.axis_index("dom")
    odd = rem(me, 2)
    rows = own.shape[0]
    width = own.shape[1]
    head = width // HEADS
    beside = lax.rem(me + 2 * odd - 1 + peers, peers)
    far = {XX: 1 << swaps[1], YY: 1 << swaps[2], ZZ: 1 << swaps[3]}
    partner = {
        CORE: flip(me, swaps[0]), XX: flip(me, swaps[1]), YY: flip(me, swaps[2]),
        HALO: beside, ZZ: flip(me, swaps[3]),
    }

    cut = 3 * peers // 4
    even = odd == 0
    bit = {k: rem(div(me, far[k]), 2) for k in (XX, YY, ZZ)}
    upper = bit[ZZ] == 1
    row, plane = 2 * far[XX], 2 * far[YY]

    def begins(who):
        return ((rem(who, row) == 0) & (rem(who, plane) > 0)) | (who == cut)

    late_halo = (odd == 1) & ((beside == 0) | begins(beside))
    beyond = me >= peers // 2

    def precedes(who, by):
        return (rem(who, plane) == plane - by) & ((upper & (rem(div(me, plane), 2) == 1)) | beyond)

    apart = precedes(me, 1)
    stands_in = precedes(me, 2)
    late = {k: (me == 0) | ((bit[k] == 1) & (me != far[k])) for k in (XX, YY)}
    barrier = pltpu.get_barrier_semaphore()

    def greet(who):
        pl.semaphore_signal(barrier, inc=1, device_id=(who,), device_id_type=MESH)

    def tell(sem, who):
        pl.semaphore_signal(sem, inc=1, device_id=(who,), device_id_type=MESH)

    @pl.when(me > 0)
    def _():
        q = partner[ZZ]
        greet(jnp.where(q == 1, 1, q - odd))
        greet(partner[CORE])
        for k in (YY, XX):
            @pl.when(jnp.logical_not(late[k]))
            def _(k=k):
                q = partner[k]
                r = q + 1 - odd
                greet(jnp.where(q == 0, 0, jnp.where(precedes(r, 1), r - 1, r)))

    @pl.when(jnp.logical_not(late_halo))
    def _():
        greet(jnp.where(precedes(me, 3), beside, beside + odd))

    pulls = [
        pltpu.make_async_copy(src, dst, local_sem.at[i])
        for i, (src, dst) in enumerate(
            ((f_hbm, own), (wq_hbm, wq), (wk_hbm, wk), (wv_hbm, wv),
             (lb_hbm, lb), (lc_hbm, lc), (eb_hbm, eb), (ec_hbm, ec))
        )
    ]
    for pull in pulls:
        pull.start()

    def move(i, src, dst, who):
        return pltpu.make_async_remote_copy(
            src_ref=src, dst_ref=dst, send_sem=send_sem.at[i], recv_sem=recv_sem.at[i],
            device_id=(who,), device_id_type=MESH,
        )

    top_half, low_half = pl.ds(0, BLK), pl.ds(BLK, BLK)
    shared = pl.ds(pl.multiple_of(odd * BLK, BLK), BLK)
    moves = [move(k, f_hbm, kv.at[k], partner[k]) for k in (CORE, XX, YY)] + [
        move(HALO, f_hbm.at[shared], kv.at[HALO, top_half], beside),
        move(ZZ, f_hbm.at[top_half], kv.at[ZZ, top_half], partner[ZZ]),
        move(ZZ + 1, f_hbm.at[low_half], kv.at[ZZ, low_half], partner[ZZ]),
    ]

    def send(k):
        moves[k].start()
        if k == ZZ:
            moves[ZZ + 1].start()

    def give_ready(mate):
        for k in (YY, XX):
            @pl.when(bit[k] == 1)
            def _(k=k):
                tell(ready_sem.at[k], partner[k])

                @pl.when(partner[k] + mate != 0)
                def _():
                    tell(ready_sem.at[k], partner[k] + mate)

    def send_late():
        for k in (YY, XX):
            @pl.when(late[k])
            def _(k=k):
                send(k)

    def even_hears():
        usual = jnp.where(stands_in, 8, 3)
        pl.semaphore_wait(barrier, jnp.where(me == 0, 4, jnp.where(me == far[ZZ], 2, usual)))

        @pl.when(me == 0)
        def _():
            for k in (ZZ, YY, XX, CORE):
                tell(ready_sem.at[k], partner[k])
            for k in (CORE, ZZ, YY, XX):
                send(k)

        @pl.when(me > 0)
        def _():
            tell(ok_sem, partner[CORE])

            @pl.when(me != far[ZZ])
            def _():
                send(ZZ)

            send(CORE)

        @pl.when(stands_in)
        def _():
            give_ready(1)
            send(HALO)
            send_late()

    def even_told():
        pl.semaphore_wait(ok_sem, 1)

        @pl.when(jnp.logical_not(begins(me)))
        def _():
            send(HALO)

        send_late()

    def odd_told():
        pl.semaphore_wait(ok_sem, 1)
        send(ZZ)

        @pl.when(apart)
        def _():
            send_late()

    def odd_hears():
        usual = 3 + 2 * bit[XX] + 2 * bit[YY]
        usual -= jnp.where((me == far[XX] + 1) | (me == far[YY] + 1), 1, 0)
        usual -= jnp.where(begins(me - 1), 1, 0)
        count = jnp.where((me == 1) | apart, 2, usual)
        pl.semaphore_wait(barrier, count)

        @pl.when(late_halo)
        def _():
            tell(ready_sem.at[HALO], beside)

        @pl.when((me > 1) & jnp.logical_not(apart))
        def _():
            tell(ok_sem, partner[CORE])
            give_ready(-1)

        @pl.when(me == 1)
        def _():
            send(ZZ)

        send(HALO)

        @pl.when(me > 1)
        def _():
            send(CORE)

        @pl.when(jnp.logical_not(apart))
        def _():
            send_late()

    corner = rem(me, plane) <= 1
    even_z_first = upper | beyond | corner
    odd_z_first = (upper | corner) & (me > 1) & jnp.logical_not(apart)

    @pl.when(even & even_z_first)
    def _():
        even_hears()

    @pl.when((odd == 1) & odd_z_first)
    def _():
        odd_told()

    @pl.when((odd == 1) & jnp.logical_not(corner))
    def _():
        odd_hears()

    @pl.when(even & jnp.logical_not(corner | stands_in))
    def _():
        even_told()

    @pl.when(even & jnp.logical_not(even_z_first))
    def _():
        even_hears()

    @pl.when((odd == 1) & (beyond | apart) & jnp.logical_not(odd_z_first))
    def _():
        odd_told()

    for i in range(4):
        pulls[i].wait()
    own_rows = own[...]
    scale = LOG2E * float(head) ** (-0.5)
    qt = (dot(wq[...], own_rows, ((0,), (1,))) * scale).astype(BF16)
    wvt[...] = wv[...].T
    for h in range(HEADS):
        parts = [qt[h * head:(h + 1) * head]]
        if h:
            parts.insert(0, jnp.zeros((h * head, rows), BF16))
        if h < HEADS - 1:
            parts.append(jnp.zeros((width - (h + 1) * head, rows), BF16))
        g[h] = dot(wk[...], jnp.concatenate(parts, axis=0), ((1,), (0,))).astype(BF16)

    @pl.when((odd == 1) & corner)
    def _():
        odd_hears()

    @pl.when(even & corner & (me > 0))
    def _():
        even_told()

    for k in (XX, YY):
        @pl.when(jnp.logical_not(late[k]) & (me != far[k]))
        def _(k=k):
            pl.semaphore_wait(ready_sem.at[k], 1)
            send(k)

    @pl.when((odd == 1) & jnp.logical_not(beyond | apart | odd_z_first) & (me > 1))
    def _():
        odd_told()

    @pl.when(begins(me) & (me != cut))
    def _():
        pl.semaphore_wait(ready_sem.at[HALO], 1)
        send(HALO)

    for i in range(4, 8):
        pulls[i].wait()

    def put(slot, block, counts):
        row = [
            jnp.full((1, BLK), jnp.where(c == 0, OFF, jnp.where(c == 1, 0.0, 1.0)).astype(F32))
            for c in counts
        ]
        bias[slot, pl.ds(block, 1), :] = jnp.concatenate(row, axis=1)

    def in_local(q, position):
        used = jnp.int32(0)
        for j in range(4):
            used += jnp.where((lb[q, j] == position) & (j < lc[q]), 1, 0)
        return used

    def in_match(m, q, block):
        used = jnp.int32(0)
        for j in range(2):
            used += jnp.where((eb[q, j, m] == block) & (j < ec[q, m]), 1, 0)
        return used

    near = [[in_local(q, j) for j in range(4)] for q in range(2)]
    for b in range(2):
        put(0, b, [near[q][1 + b] for q in range(2)])
        extra = [jnp.where(odd == b, near[q][0] if b else near[q][3], 0) for q in range(2)]
        put(1 + CORE, b, [in_match(0, q, b) + extra[q] for q in range(2)])
        for m, k in ((1, XX), (2, YY), (3, ZZ)):
            put(1 + k, b, [in_match(m, q, b) for q in range(2)])
    put(1 + HALO, 0, [jnp.where(odd == 1, near[q][3], near[q][0]) for q in range(2)])

    for h in range(HEADS):
        vt[h, pl.ds(head, 16), :] = jnp.ones((16, rows), BF16)
    top[...] = jnp.full(top.shape, FLOOR, F32)
    acc[...] = jnp.zeros(acc.shape, F32)

    def part(keys, slot, blocks):
        span = BLK * len(blocks)
        values = dot(wvt[...], keys, ((1,), (1,))).astype(BF16)
        for h in range(HEADS):
            vt[h, pl.ds(0, head), pl.ds(0, span)] = values[h * head:(h + 1) * head]
        for h in range(HEADS):
            raw[h, pl.ds(0, span)] = dot(keys, g[h], ((1,), (0,)))
        offsets = [bias[slot, pl.ds(b, 1), :] for b in blocks]
        for h in range(HEADS):
            scores = [raw[h, pl.ds(i * BLK, BLK)] for i in range(len(blocks))]
            old = top[h]
            new = old
            for score, offset in zip(scores, offsets):
                new = jnp.maximum(new, jnp.max(score, axis=0, keepdims=True) + offset)
            top[h] = new
            weights = [
                jnp.exp2(score - (new - offset)).astype(BF16)
                for score, offset in zip(scores, offsets)
            ]
            weights = jnp.concatenate(weights, axis=0) if len(blocks) > 1 else weights[0]
            out = dot(vt[h, :, pl.ds(0, span)], weights, ((1,), (0,)))
            acc[h] = acc[h] * jnp.exp2(old - new) + out[: head + 8]

    part(own_rows, 0, (0, 1))

    def answer(who, k):
        @pl.when(me == who)
        def _():
            pl.semaphore_wait(ready_sem.at[k], 1)
            send(k)

    for who, k in ((1, CORE), (far[XX], XX), (far[YY], YY), (far[ZZ], ZZ), (cut, HALO)):
        answer(who, k)

    def full(k):
        move(k, f_hbm, kv.at[k], partner[CORE]).wait_recv()
        part(kv[k], k + 1, (0, 1))

    def halo():
        moves[HALO].wait_recv()
        part(kv[HALO, top_half], 1 + HALO, (0,))

    def half(b):
        moves[ZZ + b].wait_recv()
        part(kv[ZZ, (top_half, low_half)[b]], 1 + ZZ, (b,))

    wraps = (rem(me, plane) == 0) | (rem(me, row) == row - 1)
    inner = rem(div(me, plane), 2) != bit[ZZ]

    @pl.when(me != 1)
    def _():
        full(CORE)

    @pl.when(jnp.logical_not(wraps))
    def _():
        halo()

    @pl.when(inner)
    def _():
        half(0)
        half(1)

    edge = rem(me, row) <= 1

    @pl.when(edge & jnp.logical_not(inner))
    def _():
        half(0)

    @pl.when(jnp.logical_not(corner))
    def _():
        full(YY)

    @pl.when(jnp.logical_not(edge | inner))
    def _():
        half(0)

    full(XX)

    @pl.when(jnp.logical_not(inner))
    def _():
        half(1)

    @pl.when(corner)
    def _():
        full(YY)

    @pl.when(me == 1)
    def _():
        full(CORE)

    answer(0, HALO)

    @pl.when(wraps)
    def _():
        halo()

    for h in range(HEADS):
        share = 1.0 / acc[h, pl.ds(head, 1), :]
        ctx_ref[pl.ds(h * head, head), :] = (acc[h, pl.ds(0, head), :] * share).astype(BF16)
    for i in range(MOVES):
        moves[i].wait_send()


def finish_kernel(ctx_ref, f_ref, w_ref, o_hbm, done, sem):
    rows = f_ref.shape[0]
    copies = []
    for b in range(rows // BLK):
        block = pl.ds(b * BLK, BLK)
        mixed = dot(ctx_ref[:, block], w_ref[...], ((0,), (0,)))
        mean = jnp.mean(mixed * mixed, axis=-1, keepdims=True)
        done[block, :] = (f_ref[block, :].astype(F32) + mixed * lax.rsqrt(mean + EPS)).astype(BF16)
        copies.append(pltpu.make_async_copy(done.at[block], o_hbm.at[block], sem.at[b]))
        copies[-1].start()
    for copy in copies:
        copy.wait()


def shards(features, w_query, w_key, w_value, w_out, local_blocks, local_count, expander_blocks, expander_count):
    rows, width = features.shape
    head = width // HEADS
    peers = lax.axis_size("dom")
    levels = peers.bit_length() - 1
    matches = expander_blocks.shape[0]
    swaps = [m * levels // matches for m in range(matches)]
    whole = pl.BlockSpec(memory_space=pltpu.HBM)
    inside = pl.BlockSpec(memory_space=pltpu.VMEM)
    expander_blocks = jnp.transpose(expander_blocks, (1, 2, 0))
    expander_count = expander_count.T
    ctx = pl.pallas_call(
        functools.partial(attend_kernel, peers, swaps),
        out_shape=jax.ShapeDtypeStruct((width, rows), BF16),
        in_specs=[whole] * 8,
        out_specs=inside,
        scratch_shapes=[
            pltpu.VMEM((rows, width), BF16),
            pltpu.VMEM((width, width), BF16),
            pltpu.VMEM((width, width), BF16),
            pltpu.VMEM((width, width), BF16),
            pltpu.SMEM(local_blocks.shape, jnp.int32),
            pltpu.SMEM(local_count.shape, jnp.int32),
            pltpu.SMEM(expander_blocks.shape, jnp.int32),
            pltpu.SMEM(expander_count.shape, jnp.int32),
            pltpu.VMEM((5, rows, width), BF16),
            pltpu.VMEM((HEADS, width, rows), BF16),
            pltpu.VMEM((width, width), BF16),
            pltpu.VMEM((HEADS, head + 16, rows), BF16),
            pltpu.VMEM((6, 8, rows), F32),
            pltpu.VMEM((HEADS, 1, rows), F32),
            pltpu.VMEM((HEADS, head + 8, rows), F32),
            pltpu.VMEM((HEADS, rows, rows), F32),
            pltpu.SemaphoreType.DMA((8,)),
            pltpu.SemaphoreType.DMA((MOVES,)),
            pltpu.SemaphoreType.DMA((MOVES,)),
            pltpu.SemaphoreType.REGULAR,
            pltpu.SemaphoreType.REGULAR((5,)),
        ],
        compiler_params=pltpu.CompilerParams(
            collective_id=0, has_side_effects=True, vmem_limit_bytes=32 << 20
        ),
        name="attend",
    )(*[pltpu.with_memory_space_constraint(a, pltpu.HBM) for a in (features, w_query, w_key, w_value, local_blocks, local_count, expander_blocks, expander_count)])
    return pl.pallas_call(
        finish_kernel,
        out_shape=jax.ShapeDtypeStruct((rows, width), BF16),
        in_specs=[inside] * 3,
        out_specs=whole,
        scratch_shapes=[pltpu.VMEM((rows, width), BF16), pltpu.SemaphoreType.DMA((rows // BLK,))],
        compiler_params=pltpu.CompilerParams(vmem_limit_bytes=8 << 20),
        name="finish",
    )(ctx, features, w_out)


def solution(mesh):
    in_specs = (
        P("dom", None), P(), P(), P(), P(),
        P("dom", None), P("dom"), P(None, "dom", None), P(None, "dom"),
    )
    return jax.shard_map(
        shards, mesh=mesh, in_specs=in_specs, out_specs=P("dom", None), check_vma=False
    )
```

```python
import functools

import jax
import jax.numpy as jnp
from jax import lax
from jax.experimental import pallas as pl
from jax.experimental.pallas import tpu as pltpu
from jax.sharding import PartitionSpec as P

HEADS = 8
BLK = 128
EPS = 1e-06
LOG2E = 1.4426950408889634
OFF = -1e30
FLOOR = -1e20
MESH = pl.DeviceIdType.MESH
F32 = jnp.float32
BF16 = jnp.bfloat16
CORE, XX, YY, HALO, ZZ = range(5)
MOVES = 6


def rem(a, b):
    return lax.rem(a, jnp.int32(b))


def div(a, b):
    return lax.div(a, jnp.int32(b))


def flip(me, apart):
    wide = 1 << apart
    return me + wide - 2 * wide * rem(div(me, wide), 2)


def dot(a, b, over):
    return lax.dot_general(a, b, ((over[0], over[1]), ((), ())), preferred_element_type=F32)


def attend_kernel(
    peers, swaps,
    f_hbm, wq_hbm, wk_hbm, wv_hbm, lb_hbm, lc_hbm, eb_hbm, ec_hbm,
    ctx_ref,
    own, wq, wk, wv, lb, lc, eb, ec,
    kv, g, wvt, vt, bias, top, acc, raw,
    local_sem, send_sem, recv_sem, ok_sem, ready_sem,
):
    me = lax.axis_index("dom")
    odd = rem(me, 2)
    rows = own.shape[0]
    width = own.shape[1]
    head = width // HEADS
    beside = lax.rem(me + 2 * odd - 1 + peers, peers)
    far = {XX: 1 << swaps[1], YY: 1 << swaps[2], ZZ: 1 << swaps[3]}
    partner = {
        CORE: flip(me, swaps[0]), XX: flip(me, swaps[1]), YY: flip(me, swaps[2]),
        HALO: beside, ZZ: flip(me, swaps[3]),
    }

    cut = 3 * peers // 4
    even = odd == 0
    bit = {k: rem(div(me, far[k]), 2) for k in (XX, YY, ZZ)}
    upper = bit[ZZ] == 1
    row, plane = 2 * far[XX], 2 * far[YY]

    def begins(who):
        return ((rem(who, row) == 0) & (rem(who, plane) > 0)) | (who == cut)

    late_halo = (odd == 1) & ((beside == 0) | begins(beside))
    beyond = me >= peers // 2

    def precedes(who, by):
        return (rem(who, plane) == plane - by) & ((upper & (rem(div(me, plane), 2) == 1)) | beyond)

    apart = precedes(me, 1)
    stands_in = precedes(me, 2)
    late = {k: (me == 0) | ((bit[k] == 1) & (me != far[k])) for k in (XX, YY)}
    barrier = pltpu.get_barrier_semaphore()

    def greet(who):
        pl.semaphore_signal(barrier, inc=1, device_id=(who,), device_id_type=MESH)

    def tell(sem, who):
        pl.semaphore_signal(sem, inc=1, device_id=(who,), device_id_type=MESH)

    @pl.when(me > 0)
    def _():
        q = partner[ZZ]
        greet(jnp.where(q == 1, 1, q - odd))
        greet(partner[CORE])
        for k in (YY, XX):
            @pl.when(jnp.logical_not(late[k]))
            def _(k=k):
                q = partner[k]
                r = q + 1 - odd
                greet(jnp.where(q == 0, 0, jnp.where(precedes(r, 1), r - 1, r)))

    @pl.when(jnp.logical_not(late_halo))
    def _():
        greet(jnp.where(precedes(me, 3), beside, beside + odd))

    pulls = [
        pltpu.make_async_copy(src, dst, local_sem.at[i])
        for i, (src, dst) in enumerate(
            ((f_hbm, own), (wq_hbm, wq), (wk_hbm, wk), (wv_hbm, wv),
             (lb_hbm, lb), (lc_hbm, lc), (eb_hbm, eb), (ec_hbm, ec))
        )
    ]
    for pull in pulls:
        pull.start()

    def move(i, src, dst, who):
        return pltpu.make_async_remote_copy(
            src_ref=src, dst_ref=dst, send_sem=send_sem.at[i], recv_sem=recv_sem.at[i],
            device_id=(who,), device_id_type=MESH,
        )

    top_half, low_half = pl.ds(0, BLK), pl.ds(BLK, BLK)
    shared = pl.ds(pl.multiple_of(odd * BLK, BLK), BLK)
    moves = [move(k, f_hbm, kv.at[k], partner[k]) for k in (CORE, XX, YY)] + [
        move(HALO, f_hbm.at[shared], kv.at[HALO, top_half], beside),
        move(ZZ, f_hbm.at[top_half], kv.at[ZZ, top_half], partner[ZZ]),
        move(ZZ + 1, f_hbm.at[low_half], kv.at[ZZ, low_half], partner[ZZ]),
    ]

    def send(k):
        moves[k].start()
        if k == ZZ:
            moves[ZZ + 1].start()

    def give_ready(mate):
        for k in (YY, XX):
            @pl.when(bit[k] == 1)
            def _(k=k):
                tell(ready_sem.at[k], partner[k])

                @pl.when(partner[k] + mate != 0)
                def _():
                    tell(ready_sem.at[k], partner[k] + mate)

    def send_late():
        for k in (YY, XX):
            @pl.when(late[k])
            def _(k=k):
                send(k)

    def even_hears():
        usual = jnp.where(stands_in, 8, 3)
        pl.semaphore_wait(barrier, jnp.where(me == 0, 4, jnp.where(me == far[ZZ], 2, usual)))

        @pl.when(me == 0)
        def _():
            for k in (ZZ, YY, XX, CORE):
                tell(ready_sem.at[k], partner[k])
            for k in (CORE, ZZ, YY, XX):
                send(k)

        @pl.when(me > 0)
        def _():
            tell(ok_sem, partner[CORE])

            @pl.when(me != far[ZZ])
            def _():
                send(ZZ)

            send(CORE)

        @pl.when(stands_in)
        def _():
            give_ready(1)
            send(HALO)
            send_late()

    def even_told():
        pl.semaphore_wait(ok_sem, 1)

        @pl.when(jnp.logical_not(begins(me)))
        def _():
            send(HALO)

        send_late()

    def odd_told():
        pl.semaphore_wait(ok_sem, 1)
        send(ZZ)

        @pl.when(apart)
        def _():
            send_late()

    def odd_hears():
        usual = 3 + 2 * bit[XX] + 2 * bit[YY]
        usual -= jnp.where((me == far[XX] + 1) | (me == far[YY] + 1), 1, 0)
        usual -= jnp.where(begins(me - 1), 1, 0)
        count = jnp.where((me == 1) | apart, 2, usual)
        pl.semaphore_wait(barrier, count)

        @pl.when(late_halo)
        def _():
            tell(ready_sem.at[HALO], beside)

        @pl.when((me > 1) & jnp.logical_not(apart))
        def _():
            tell(ok_sem, partner[CORE])
            give_ready(-1)

        @pl.when(me == 1)
        def _():
            send(ZZ)

        send(HALO)

        @pl.when(me > 1)
        def _():
            send(CORE)

        @pl.when(jnp.logical_not(apart))
        def _():
            send_late()

    corner = rem(me, plane) <= 1
    even_z_first = upper | beyond | corner
    odd_z_first = (upper | corner) & (me > 1) & jnp.logical_not(apart)

    @pl.when(even & even_z_first)
    def _():
        even_hears()

    @pl.when((odd == 1) & odd_z_first)
    def _():
        odd_told()

    @pl.when((odd == 1) & jnp.logical_not(corner))
    def _():
        odd_hears()

    @pl.when(even & jnp.logical_not(corner | stands_in))
    def _():
        even_told()

    @pl.when(even & jnp.logical_not(even_z_first))
    def _():
        even_hears()

    @pl.when((odd == 1) & (beyond | apart) & jnp.logical_not(odd_z_first))
    def _():
        odd_told()

    for i in range(4):
        pulls[i].wait()
    own_rows = own[...]
    scale = LOG2E * float(head) ** (-0.5)
    qt = (dot(wq[...], own_rows, ((0,), (1,))) * scale).astype(BF16)
    wvt[...] = wv[...].T
    for h in range(HEADS):
        parts = [qt[h * head:(h + 1) * head]]
        if h:
            parts.insert(0, jnp.zeros((h * head, rows), BF16))
        if h < HEADS - 1:
            parts.append(jnp.zeros((width - (h + 1) * head, rows), BF16))
        g[h] = dot(wk[...], jnp.concatenate(parts, axis=0), ((1,), (0,))).astype(BF16)

    @pl.when((odd == 1) & corner)
    def _():
        odd_hears()

    @pl.when(even & corner & (me > 0))
    def _():
        even_told()

    for k in (XX, YY):
        @pl.when(jnp.logical_not(late[k]) & (me != far[k]))
        def _(k=k):
            pl.semaphore_wait(ready_sem.at[k], 1)
            send(k)

    @pl.when((odd == 1) & jnp.logical_not(beyond | apart | odd_z_first) & (me > 1))
    def _():
        odd_told()

    @pl.when(begins(me) & (me != cut))
    def _():
        pl.semaphore_wait(ready_sem.at[HALO], 1)
        send(HALO)

    for i in range(4, 8):
        pulls[i].wait()

    def put(slot, block, counts):
        row = [
            jnp.full((1, BLK), jnp.where(c == 0, OFF, jnp.where(c == 1, 0.0, 1.0)).astype(F32))
            for c in counts
        ]
        bias[slot, pl.ds(block, 1), :] = jnp.concatenate(row, axis=1)

    def in_local(q, position):
        used = jnp.int32(0)
        for j in range(4):
            used += jnp.where((lb[q, j] == position) & (j < lc[q]), 1, 0)
        return used

    def in_match(m, q, block):
        used = jnp.int32(0)
        for j in range(2):
            used += jnp.where((eb[q, j, m] == block) & (j < ec[q, m]), 1, 0)
        return used

    near = [[in_local(q, j) for j in range(4)] for q in range(2)]
    for b in range(2):
        put(0, b, [near[q][1 + b] for q in range(2)])
        extra = [jnp.where(odd == b, near[q][0] if b else near[q][3], 0) for q in range(2)]
        put(1 + CORE, b, [in_match(0, q, b) + extra[q] for q in range(2)])
        for m, k in ((1, XX), (2, YY), (3, ZZ)):
            put(1 + k, b, [in_match(m, q, b) for q in range(2)])
    put(1 + HALO, 0, [jnp.where(odd == 1, near[q][3], near[q][0]) for q in range(2)])

    for h in range(HEADS):
        vt[h, pl.ds(head, 16), :] = jnp.ones((16, rows), BF16)
    top[...] = jnp.full(top.shape, FLOOR, F32)
    acc[...] = jnp.zeros(acc.shape, F32)

    def part(keys, slot, blocks):
        span = BLK * len(blocks)
        values = dot(wvt[...], keys, ((1,), (1,))).astype(BF16)
        for h in range(HEADS):
            vt[h, pl.ds(0, head), pl.ds(0, span)] = values[h * head:(h + 1) * head]
        for h in range(HEADS):
            raw[h, pl.ds(0, span)] = dot(keys, g[h], ((1,), (0,)))
        offsets = [bias[slot, pl.ds(b, 1), :] for b in blocks]
        for h in range(HEADS):
            scores = [raw[h, pl.ds(i * BLK, BLK)] for i in range(len(blocks))]
            old = top[h]
            new = old
            for score, offset in zip(scores, offsets):
                new = jnp.maximum(new, jnp.max(score, axis=0, keepdims=True) + offset)
            top[h] = new
            weights = [
                jnp.exp2(score - (new - offset)).astype(BF16)
                for score, offset in zip(scores, offsets)
            ]
            weights = jnp.concatenate(weights, axis=0) if len(blocks) > 1 else weights[0]
            out = dot(vt[h, :, pl.ds(0, span)], weights, ((1,), (0,)))
            acc[h] = acc[h] * jnp.exp2(old - new) + out[: head + 8]

    part(own_rows, 0, (0, 1))

    def answer(who, k):
        @pl.when(me == who)
        def _():
            pl.semaphore_wait(ready_sem.at[k], 1)
            send(k)

    for who, k in ((1, CORE), (far[XX], XX), (far[YY], YY), (far[ZZ], ZZ), (cut, HALO)):
        answer(who, k)

    def full(k):
        move(k, f_hbm, kv.at[k], partner[CORE]).wait_recv()
        part(kv[k], k + 1, (0, 1))

    def halo():
        moves[HALO].wait_recv()
        part(kv[HALO, top_half], 1 + HALO, (0,))

    def half(b):
        moves[ZZ + b].wait_recv()
        part(kv[ZZ, (top_half, low_half)[b]], 1 + ZZ, (b,))

    wraps = (rem(me, plane) == 0) | (rem(me, row) == row - 1)
    inner = rem(div(me, plane), 2) != bit[ZZ]

    @pl.when(me != 1)
    def _():
        full(CORE)

    @pl.when(jnp.logical_not(wraps))
    def _():
        halo()

    @pl.when(inner)
    def _():
        half(0)
        half(1)

    edge = (rem(me, row) <= 1) | (odd == 1) | upper

    @pl.when(edge & jnp.logical_not(inner))
    def _():
        half(0)

    @pl.when(jnp.logical_not(corner))
    def _():
        full(YY)

    @pl.when(jnp.logical_not(edge | inner))
    def _():
        half(0)

    full(XX)

    @pl.when(jnp.logical_not(inner))
    def _():
        half(1)

    @pl.when(corner)
    def _():
        full(YY)

    @pl.when(me == 1)
    def _():
        full(CORE)

    answer(0, HALO)

    @pl.when(wraps)
    def _():
        halo()

    for h in range(HEADS):
        share = 1.0 / acc[h, pl.ds(head, 1), :]
        ctx_ref[pl.ds(h * head, head), :] = (acc[h, pl.ds(0, head), :] * share).astype(BF16)
    for i in range(MOVES):
        moves[i].wait_send()


def finish_kernel(ctx_ref, f_ref, w_ref, o_hbm, done, sem):
    rows = f_ref.shape[0]
    copies = []
    for b in range(rows // BLK):
        block = pl.ds(b * BLK, BLK)
        mixed = dot(ctx_ref[:, block], w_ref[...], ((0,), (0,)))
        mean = jnp.mean(mixed * mixed, axis=-1, keepdims=True)
        done[block, :] = (f_ref[block, :].astype(F32) + mixed * lax.rsqrt(mean + EPS)).astype(BF16)
        copies.append(pltpu.make_async_copy(done.at[block], o_hbm.at[block], sem.at[b]))
        copies[-1].start()
    for copy in copies:
        copy.wait()


def shards(features, w_query, w_key, w_value, w_out, local_blocks, local_count, expander_blocks, expander_count):
    rows, width = features.shape
    head = width // HEADS
    peers = lax.axis_size("dom")
    levels = peers.bit_length() - 1
    matches = expander_blocks.shape[0]
    swaps = [m * levels // matches for m in range(matches)]
    whole = pl.BlockSpec(memory_space=pltpu.HBM)
    inside = pl.BlockSpec(memory_space=pltpu.VMEM)
    expander_blocks = jnp.transpose(expander_blocks, (1, 2, 0))
    expander_count = expander_count.T
    ctx = pl.pallas_call(
        functools.partial(attend_kernel, peers, swaps),
        out_shape=jax.ShapeDtypeStruct((width, rows), BF16),
        in_specs=[whole] * 8,
        out_specs=inside,
        scratch_shapes=[
            pltpu.VMEM((rows, width), BF16),
            pltpu.VMEM((width, width), BF16),
            pltpu.VMEM((width, width), BF16),
            pltpu.VMEM((width, width), BF16),
            pltpu.SMEM(local_blocks.shape, jnp.int32),
            pltpu.SMEM(local_count.shape, jnp.int32),
            pltpu.SMEM(expander_blocks.shape, jnp.int32),
            pltpu.SMEM(expander_count.shape, jnp.int32),
            pltpu.VMEM((5, rows, width), BF16),
            pltpu.VMEM((HEADS, width, rows), BF16),
            pltpu.VMEM((width, width), BF16),
            pltpu.VMEM((HEADS, head + 16, rows), BF16),
            pltpu.VMEM((6, 8, rows), F32),
            pltpu.VMEM((HEADS, 1, rows), F32),
            pltpu.VMEM((HEADS, head + 8, rows), F32),
            pltpu.VMEM((HEADS, rows, rows), F32),
            pltpu.SemaphoreType.DMA((8,)),
            pltpu.SemaphoreType.DMA((MOVES,)),
            pltpu.SemaphoreType.DMA((MOVES,)),
            pltpu.SemaphoreType.REGULAR,
            pltpu.SemaphoreType.REGULAR((5,)),
        ],
        compiler_params=pltpu.CompilerParams(
            collective_id=0, has_side_effects=True, vmem_limit_bytes=32 << 20
        ),
        name="attend",
    )(*[pltpu.with_memory_space_constraint(a, pltpu.HBM) for a in (features, w_query, w_key, w_value, local_blocks, local_count, expander_blocks, expander_count)])
    return pl.pallas_call(
        finish_kernel,
        out_shape=jax.ShapeDtypeStruct((rows, width), BF16),
        in_specs=[inside] * 3,
        out_specs=whole,
        scratch_shapes=[pltpu.VMEM((rows, width), BF16), pltpu.SemaphoreType.DMA((rows // BLK,))],
        compiler_params=pltpu.CompilerParams(vmem_limit_bytes=8 << 20),
        name="finish",
    )(ctx, features, w_out)


def solution(mesh):
    in_specs = (
        P("dom", None), P(), P(), P(), P(),
        P("dom", None), P("dom"), P(None, "dom", None), P(None, "dom"),
    )
    return jax.shard_map(
        shards, mesh=mesh, in_specs=in_specs, out_specs=P("dom", None), check_vma=False
    )
```

```python
import functools

import jax
import jax.numpy as jnp
from jax import lax
from jax.experimental import pallas as pl
from jax.experimental.pallas import tpu as pltpu
from jax.sharding import PartitionSpec as P

HEADS = 8
BLK = 128
EPS = 1e-06
LOG2E = 1.4426950408889634
OFF = -1e30
FLOOR = -1e20
MESH = pl.DeviceIdType.MESH
F32 = jnp.float32
BF16 = jnp.bfloat16
CORE, XX, YY, HALO, ZZ = range(5)
MOVES = 6


def rem(a, b):
    return lax.rem(a, jnp.int32(b))


def div(a, b):
    return lax.div(a, jnp.int32(b))


def flip(me, apart):
    wide = 1 << apart
    return me + wide - 2 * wide * rem(div(me, wide), 2)


def dot(a, b, over):
    return lax.dot_general(a, b, ((over[0], over[1]), ((), ())), preferred_element_type=F32)


def attend_kernel(
    peers, swaps,
    f_hbm, wq_hbm, wk_hbm, wv_hbm, lb_hbm, lc_hbm, eb_hbm, ec_hbm,
    ctx_ref,
    own, wq, wk, wv, lb, lc, eb, ec,
    kv, g, wvt, vt, bias, top, acc, raw,
    local_sem, send_sem, recv_sem, ok_sem, ready_sem,
):
    me = lax.axis_index("dom")
    odd = rem(me, 2)
    rows = own.shape[0]
    width = own.shape[1]
    head = width // HEADS
    beside = lax.rem(me + 2 * odd - 1 + peers, peers)
    far = {XX: 1 << swaps[1], YY: 1 << swaps[2], ZZ: 1 << swaps[3]}
    partner = {
        CORE: flip(me, swaps[0]), XX: flip(me, swaps[1]), YY: flip(me, swaps[2]),
        HALO: beside, ZZ: flip(me, swaps[3]),
    }

    cut = 3 * peers // 4
    even = odd == 0
    bit = {k: rem(div(me, far[k]), 2) for k in (XX, YY, ZZ)}
    upper = bit[ZZ] == 1
    row, plane = 2 * far[XX], 2 * far[YY]

    def begins(who):
        return ((rem(who, row) == 0) & (rem(who, plane) > 0)) | (who == cut)

    late_halo = (odd == 1) & ((beside == 0) | begins(beside))
    beyond = me >= peers // 2

    def precedes(who, by):
        return (rem(who, plane) == plane - by) & ((upper & (rem(div(me, plane), 2) == 1)) | beyond)

    apart = precedes(me, 1)
    stands_in = precedes(me, 2)
    late = {k: (me == 0) | ((bit[k] == 1) & (me != far[k])) for k in (XX, YY)}
    barrier = pltpu.get_barrier_semaphore()

    def greet(who):
        pl.semaphore_signal(barrier, inc=1, device_id=(who,), device_id_type=MESH)

    def tell(sem, who):
        pl.semaphore_signal(sem, inc=1, device_id=(who,), device_id_type=MESH)

    @pl.when(me > 0)
    def _():
        q = partner[ZZ]
        greet(jnp.where(q == 1, 1, q - odd))
        greet(partner[CORE])
        for k in (YY, XX):
            @pl.when(jnp.logical_not(late[k]))
            def _(k=k):
                q = partner[k]
                r = q + 1 - odd
                greet(jnp.where(q == 0, 0, jnp.where(precedes(r, 1), r - 1, r)))

    @pl.when(jnp.logical_not(late_halo))
    def _():
        greet(jnp.where(precedes(me, 3), beside, beside + odd))

    pulls = [
        pltpu.make_async_copy(src, dst, local_sem.at[i])
        for i, (src, dst) in enumerate(
            ((f_hbm, own), (wq_hbm, wq), (wk_hbm, wk), (wv_hbm, wv),
             (lb_hbm, lb), (lc_hbm, lc), (eb_hbm, eb), (ec_hbm, ec))
        )
    ]
    for pull in pulls:
        pull.start()

    def move(i, src, dst, who):
        return pltpu.make_async_remote_copy(
            src_ref=src, dst_ref=dst, send_sem=send_sem.at[i], recv_sem=recv_sem.at[i],
            device_id=(who,), device_id_type=MESH,
        )

    top_half, low_half = pl.ds(0, BLK), pl.ds(BLK, BLK)
    shared = pl.ds(pl.multiple_of(odd * BLK, BLK), BLK)
    moves = [move(k, f_hbm, kv.at[k], partner[k]) for k in (CORE, XX, YY)] + [
        move(HALO, f_hbm.at[shared], kv.at[HALO, top_half], beside),
        move(ZZ, f_hbm.at[top_half], kv.at[ZZ, top_half], partner[ZZ]),
        move(ZZ + 1, f_hbm.at[low_half], kv.at[ZZ, low_half], partner[ZZ]),
    ]

    def send(k):
        moves[k].start()
        if k == ZZ:
            moves[ZZ + 1].start()

    def give_ready(mate):
        for k in (YY, XX):
            @pl.when(bit[k] == 1)
            def _(k=k):
                tell(ready_sem.at[k], partner[k])

                @pl.when(partner[k] + mate != 0)
                def _():
                    tell(ready_sem.at[k], partner[k] + mate)

    def send_late():
        for k in (YY, XX):
            @pl.when(late[k])
            def _(k=k):
                send(k)

    def even_hears():
        usual = jnp.where(stands_in, 8, 3)
        pl.semaphore_wait(barrier, jnp.where(me == 0, 4, jnp.where(me == far[ZZ], 2, usual)))

        @pl.when(me == 0)
        def _():
            for k in (ZZ, YY, XX, CORE):
                tell(ready_sem.at[k], partner[k])
            for k in (CORE, ZZ, YY, XX):
                send(k)

        @pl.when(me > 0)
        def _():
            tell(ok_sem, partner[CORE])

            @pl.when(me != far[ZZ])
            def _():
                send(ZZ)

            send(CORE)

        @pl.when(stands_in)
        def _():
            give_ready(1)
            send(HALO)
            send_late()

    def even_told():
        pl.semaphore_wait(ok_sem, 1)

        send_late()

        @pl.when(jnp.logical_not(begins(me)))
        def _():
            send(HALO)

    def odd_told():
        pl.semaphore_wait(ok_sem, 1)
        send(ZZ)

        @pl.when(apart)
        def _():
            send_late()

    def odd_hears():
        usual = 3 + 2 * bit[XX] + 2 * bit[YY]
        usual -= jnp.where((me == far[XX] + 1) | (me == far[YY] + 1), 1, 0)
        usual -= jnp.where(begins(me - 1), 1, 0)
        count = jnp.where((me == 1) | apart, 2, usual)
        pl.semaphore_wait(barrier, count)

        @pl.when(late_halo)
        def _():
            tell(ready_sem.at[HALO], beside)

        @pl.when((me > 1) & jnp.logical_not(apart))
        def _():
            tell(ok_sem, partner[CORE])
            give_ready(-1)

        @pl.when(me == 1)
        def _():
            send(ZZ)

        send(HALO)

        @pl.when(jnp.logical_not(apart))
        def _():
            send_late()

        @pl.when(me > 1)
        def _():
            send(CORE)

    corner = rem(me, plane) <= 1
    even_z_first = upper | beyond | corner
    odd_z_first = (upper | corner) & (me > 1) & jnp.logical_not(apart)

    @pl.when(even & even_z_first)
    def _():
        even_hears()

    @pl.when((odd == 1) & odd_z_first)
    def _():
        odd_told()

    @pl.when((odd == 1) & jnp.logical_not(corner))
    def _():
        odd_hears()

    @pl.when(even & jnp.logical_not(corner | stands_in))
    def _():
        even_told()

    @pl.when(even & jnp.logical_not(even_z_first))
    def _():
        even_hears()

    @pl.when((odd == 1) & (beyond | apart) & jnp.logical_not(odd_z_first))
    def _():
        odd_told()

    for i in range(4):
        pulls[i].wait()
    own_rows = own[...]
    scale = LOG2E * float(head) ** (-0.5)
    qt = (dot(wq[...], own_rows, ((0,), (1,))) * scale).astype(BF16)
    wvt[...] = wv[...].T
    for h in range(HEADS):
        parts = [qt[h * head:(h + 1) * head]]
        if h:
            parts.insert(0, jnp.zeros((h * head, rows), BF16))
        if h < HEADS - 1:
            parts.append(jnp.zeros((width - (h + 1) * head, rows), BF16))
        g[h] = dot(wk[...], jnp.concatenate(parts, axis=0), ((1,), (0,))).astype(BF16)

    @pl.when((odd == 1) & corner)
    def _():
        odd_hears()

    @pl.when(even & corner & (me > 0))
    def _():
        even_told()

    for k in (XX, YY):
        @pl.when(jnp.logical_not(late[k]) & (me != far[k]))
        def _(k=k):
            pl.semaphore_wait(ready_sem.at[k], 1)
            send(k)

    @pl.when((odd == 1) & jnp.logical_not(beyond | apart | odd_z_first) & (me > 1))
    def _():
        odd_told()

    @pl.when(begins(me) & (me != cut))
    def _():
        pl.semaphore_wait(ready_sem.at[HALO], 1)
        send(HALO)

    for i in range(4, 8):
        pulls[i].wait()

    def put(slot, block, counts):
        row = [
            jnp.full((1, BLK), jnp.where(c == 0, OFF, jnp.where(c == 1, 0.0, 1.0)).astype(F32))
            for c in counts
        ]
        bias[slot, pl.ds(block, 1), :] = jnp.concatenate(row, axis=1)

    def in_local(q, position):
        used = jnp.int32(0)
        for j in range(4):
            used += jnp.where((lb[q, j] == position) & (j < lc[q]), 1, 0)
        return used

    def in_match(m, q, block):
        used = jnp.int32(0)
        for j in range(2):
            used += jnp.where((eb[q, j, m] == block) & (j < ec[q, m]), 1, 0)
        return used

    near = [[in_local(q, j) for j in range(4)] for q in range(2)]
    for b in range(2):
        put(0, b, [near[q][1 + b] for q in range(2)])
        extra = [jnp.where(odd == b, near[q][0] if b else near[q][3], 0) for q in range(2)]
        put(1 + CORE, b, [in_match(0, q, b) + extra[q] for q in range(2)])
        for m, k in ((1, XX), (2, YY), (3, ZZ)):
            put(1 + k, b, [in_match(m, q, b) for q in range(2)])
    put(1 + HALO, 0, [jnp.where(odd == 1, near[q][3], near[q][0]) for q in range(2)])

    for h in range(HEADS):
        vt[h, pl.ds(head, 16), :] = jnp.ones((16, rows), BF16)
    top[...] = jnp.full(top.shape, FLOOR, F32)
    acc[...] = jnp.zeros(acc.shape, F32)

    def part(keys, slot, blocks):
        span = BLK * len(blocks)
        values = dot(wvt[...], keys, ((1,), (1,))).astype(BF16)
        for h in range(HEADS):
            vt[h, pl.ds(0, head), pl.ds(0, span)] = values[h * head:(h + 1) * head]
        for h in range(HEADS):
            raw[h, pl.ds(0, span)] = dot(keys, g[h], ((1,), (0,)))
        offsets = [bias[slot, pl.ds(b, 1), :] for b in blocks]
        for h in range(HEADS):
            scores = [raw[h, pl.ds(i * BLK, BLK)] for i in range(len(blocks))]
            old = top[h]
            new = old
            for score, offset in zip(scores, offsets):
                new = jnp.maximum(new, jnp.max(score, axis=0, keepdims=True) + offset)
            top[h] = new
            weights = [
                jnp.exp2(score - (new - offset)).astype(BF16)
                for score, offset in zip(scores, offsets)
            ]
            weights = jnp.concatenate(weights, axis=0) if len(blocks) > 1 else weights[0]
            out = dot(vt[h, :, pl.ds(0, span)], weights, ((1,), (0,)))
            acc[h] = acc[h] * jnp.exp2(old - new) + out[: head + 8]

    part(own_rows, 0, (0, 1))

    def answer(who, k):
        @pl.when(me == who)
        def _():
            pl.semaphore_wait(ready_sem.at[k], 1)
            send(k)

    for who, k in ((1, CORE), (far[XX], XX), (far[YY], YY), (far[ZZ], ZZ), (cut, HALO)):
        answer(who, k)

    def full(k):
        move(k, f_hbm, kv.at[k], partner[CORE]).wait_recv()
        part(kv[k], k + 1, (0, 1))

    def halo():
        moves[HALO].wait_recv()
        part(kv[HALO, top_half], 1 + HALO, (0,))

    def half(b):
        moves[ZZ + b].wait_recv()
        part(kv[ZZ, (top_half, low_half)[b]], 1 + ZZ, (b,))

    wraps = (rem(me, plane) == 0) | (rem(me, row) == row - 1)
    inner = rem(div(me, plane), 2) != bit[ZZ]

    @pl.when(me != 1)
    def _():
        full(CORE)

    @pl.when(jnp.logical_not(wraps))
    def _():
        halo()

    @pl.when(inner)
    def _():
        half(0)
        half(1)

    edge = (rem(me, row) <= 1) | (odd == 1) | upper

    @pl.when(edge & jnp.logical_not(inner))
    def _():
        half(0)

    @pl.when(jnp.logical_not(corner))
    def _():
        full(YY)

    @pl.when(jnp.logical_not(edge | inner))
    def _():
        half(0)

    full(XX)

    @pl.when(jnp.logical_not(inner))
    def _():
        half(1)

    @pl.when(corner)
    def _():
        full(YY)

    @pl.when(me == 1)
    def _():
        full(CORE)

    answer(0, HALO)

    @pl.when(wraps)
    def _():
        halo()

    for h in range(HEADS):
        share = 1.0 / acc[h, pl.ds(head, 1), :]
        ctx_ref[pl.ds(h * head, head), :] = (acc[h, pl.ds(0, head), :] * share).astype(BF16)
    for i in range(MOVES):
        moves[i].wait_send()


def finish_kernel(ctx_ref, f_ref, w_ref, o_hbm, done, sem):
    rows = f_ref.shape[0]
    copies = []
    for b in range(rows // BLK):
        block = pl.ds(b * BLK, BLK)
        mixed = dot(ctx_ref[:, block], w_ref[...], ((0,), (0,)))
        mean = jnp.mean(mixed * mixed, axis=-1, keepdims=True)
        done[block, :] = (f_ref[block, :].astype(F32) + mixed * lax.rsqrt(mean + EPS)).astype(BF16)
        copies.append(pltpu.make_async_copy(done.at[block], o_hbm.at[block], sem.at[b]))
        copies[-1].start()
    for copy in copies:
        copy.wait()


def shards(features, w_query, w_key, w_value, w_out, local_blocks, local_count, expander_blocks, expander_count):
    rows, width = features.shape
    head = width // HEADS
    peers = lax.axis_size("dom")
    levels = peers.bit_length() - 1
    matches = expander_blocks.shape[0]
    swaps = [m * levels // matches for m in range(matches)]
    whole = pl.BlockSpec(memory_space=pltpu.HBM)
    inside = pl.BlockSpec(memory_space=pltpu.VMEM)
    expander_blocks = jnp.transpose(expander_blocks, (1, 2, 0))
    expander_count = expander_count.T
    ctx = pl.pallas_call(
        functools.partial(attend_kernel, peers, swaps),
        out_shape=jax.ShapeDtypeStruct((width, rows), BF16),
        in_specs=[whole] * 8,
        out_specs=inside,
        scratch_shapes=[
            pltpu.VMEM((rows, width), BF16),
            pltpu.VMEM((width, width), BF16),
            pltpu.VMEM((width, width), BF16),
            pltpu.VMEM((width, width), BF16),
            pltpu.SMEM(local_blocks.shape, jnp.int32),
            pltpu.SMEM(local_count.shape, jnp.int32),
            pltpu.SMEM(expander_blocks.shape, jnp.int32),
            pltpu.SMEM(expander_count.shape, jnp.int32),
            pltpu.VMEM((5, rows, width), BF16),
            pltpu.VMEM((HEADS, width, rows), BF16),
            pltpu.VMEM((width, width), BF16),
            pltpu.VMEM((HEADS, head + 16, rows), BF16),
            pltpu.VMEM((6, 8, rows), F32),
            pltpu.VMEM((HEADS, 1, rows), F32),
            pltpu.VMEM((HEADS, head + 8, rows), F32),
            pltpu.VMEM((HEADS, rows, rows), F32),
            pltpu.SemaphoreType.DMA((8,)),
            pltpu.SemaphoreType.DMA((MOVES,)),
            pltpu.SemaphoreType.DMA((MOVES,)),
            pltpu.SemaphoreType.REGULAR,
            pltpu.SemaphoreType.REGULAR((5,)),
        ],
        compiler_params=pltpu.CompilerParams(
            collective_id=0, has_side_effects=True, vmem_limit_bytes=32 << 20
        ),
        name="attend",
    )(*[pltpu.with_memory_space_constraint(a, pltpu.HBM) for a in (features, w_query, w_key, w_value, local_blocks, local_count, expander_blocks, expander_count)])
    return pl.pallas_call(
        finish_kernel,
        out_shape=jax.ShapeDtypeStruct((rows, width), BF16),
        in_specs=[inside] * 3,
        out_specs=whole,
        scratch_shapes=[pltpu.VMEM((rows, width), BF16), pltpu.SemaphoreType.DMA((rows // BLK,))],
        compiler_params=pltpu.CompilerParams(vmem_limit_bytes=8 << 20),
        name="finish",
    )(ctx, features, w_out)


def solution(mesh):
    in_specs = (
        P("dom", None), P(), P(), P(), P(),
        P("dom", None), P("dom"), P(None, "dom", None), P(None, "dom"),
    )
    return jax.shard_map(
        shards, mesh=mesh, in_specs=in_specs, out_specs=P("dom", None), check_vma=False
    )
```
